256 devices in a mesh: layer: 8 (over z_lo, core), feat: 32 (over x, y, z_hi).
Axes of the slice: x: 4, y: 4, z: 8 (z_hi: 2, z_lo: 4; z = z_hi * 4 + z_lo), core: 2. Of those that a mesh axis runs over, the one named last changes fastest.
Arguments:
- source: bfloat16 [512, 2304], P('feat', 'layer'), may hold values from -6 to 6
- enc_weight: bfloat16 [2304, 32768], P('layer', 'feat'), may hold values from -0.125 to 0.125
- enc_bias: float32 [32768], P('feat'), may hold values from -3 to 3
- dec_weight: bfloat16 [8, 32768, 2304], P('layer', 'feat'), may hold values from -0.03125 to 0.03125
- dec_bias: float32 [8, 2304], P('layer'), may hold values from -3 to 3
- targets: bfloat16 [8, 512, 2304], P('layer', 'feat'), may hold values from -6 to 6
Outputs:
- enc_grad: bfloat16 [2304, 32768], P('layer', 'feat')
- dec_grad: bfloat16 [8, 32768, 2304], P('layer', 'feat')
The draws below stay inside these ranges and needn't reach their ends.
All inputs are finite; a program needn't handle non-finite values.
Results may differ from the reference program's by a relative error of at most 0.014.
Values may be sent and summed in bfloat16 or wider, within the bound.
A program may use at most 64 MiB of HBM per device.

```python
import jax
import jax.numpy as jnp
from jax import lax

D = 2304
F = 32768
TOKENS = 512
LAYERS = 8


def level_of(rng, dims, split, least, largest):
    def one(dim, blocks):
        heights = jax.random.uniform(jax.random.fold_in(jax.random.fold_in(rng, 6), dim), (blocks,), jnp.float32, least / len(split), largest / len(split))
        return jnp.repeat(jnp.exp(heights), dims[dim] // blocks).reshape((-1,) + (1,) * (len(dims) - dim - 1))

    loudness = one(*split[0])
    for cut in split[1:]:
        loudness = loudness * one(*cut)
    return loudness


def gaussian(rng, extent, deviation, limit, pieces=(), kind=jnp.bfloat16):
    result = deviation * jax.random.normal(rng, extent, jnp.float32)
    if pieces:
        result = result * level_of(rng, extent, pieces, -0.22, 0.18)
    return jnp.clip(result, -limit, limit).astype(kind)


def setup_inputs(seed: int = 0) -> dict:
    key_list = jax.random.split(jax.random.key(seed), 7)
    return {
        "source": gaussian(key_list[0], (TOKENS, D), 1.0, 6.0, ((0, 32), (1, 8))),
        "enc_weight": gaussian(key_list[1], (D, F), D ** -0.5, 0.125, ((0, 8), (1, 32))),
        "enc_bias": gaussian(key_list[2], (F,), 0.5, 3.0, ((0, 32),), jnp.float32),
        "dec_weight": gaussian(key_list[3], (LAYERS, F, D), F ** -0.5, 0.03125, ((0, 8), (1, 32))),
        "dec_bias": gaussian(key_list[4], (LAYERS, D), 0.5, 3.0, ((0, 8),), jnp.float32),
        "targets": gaussian(key_list[5], (LAYERS, TOKENS, D), 1.0, 6.0, ((0, 8), (1, 32))),
    }


def reference(source, enc_weight, enc_bias, dec_weight, dec_bias, targets):
    preact = jnp.dot(source, enc_weight, preferred_element_type=jnp.float32) + enc_bias[None, :]
    active = jnp.maximum(preact, 0.0)
    features = (active * active).astype(jnp.bfloat16)

    def per_layer(carry, inputs):
        decoder, bias, target = inputs
        rebuilt = jnp.dot(features, decoder, preferred_element_type=jnp.float32) + bias[None, :]
        residual = (rebuilt - target.astype(jnp.float32)).astype(jnp.bfloat16)
        weight_grad = jnp.dot(features.T, residual, preferred_element_type=jnp.float32).astype(jnp.bfloat16)
        carry = carry + lax.dot_general(residual, decoder, (((1,), (1,)), ((), ())), preferred_element_type=jnp.float32)
        return carry, weight_grad

    initial = jnp.zeros(preact.shape, jnp.float32)
    summed, dec_grad = lax.scan(per_layer, initial, (dec_weight, dec_bias, targets))
    feat_grad = (2.0 * active * summed).astype(jnp.bfloat16)
    enc_grad = jnp.dot(source.T, feat_grad, preferred_element_type=jnp.float32).astype(jnp.bfloat16)
    return enc_grad, dec_grad
```

```python
import functools

import jax
import jax.numpy as jnp
from jax import lax
from jax.experimental import pallas as pl
from jax.experimental.pallas import tpu as pltpu
from jax.sharding import PartitionSpec as P

MESH = pl.DeviceIdType.MESH
F32 = jnp.float32
BF16 = jnp.bfloat16

D = 2304
HD = D // 2
NF = 1024
HF = NF // 2
KD = 288
KP = 384
CH = 256
TILES = ((0, 256), (256, 256), (512, 256), (768, 256), (1024, 128))


def dot(a, b):
    return jnp.dot(a, b, preferred_element_type=F32)


def dot_nt(a, b):
    return lax.dot_general(a, b, (((1,), (1,)), ((), ())), preferred_element_type=F32)


class Ids:
    def __init__(self):
        self.table = {}

    def __getitem__(self, name):
        return self.table.setdefault(name, len(self.table))


N_SEM = 200


def kernel(src_ref, encw_ref, bias_ref, decw_ref, dbias_ref, tgt_ref, eg_ref, dg_ref,
           srcb, wenc, w, tg, pown, xs, xr, zs, zr, act, feats, feat_t, src_t, fgr, egacc,
           rb, t1, t2, qs, qr, us, ur, res, stag, egout, ssem, rsem, lsem):
    layer = lax.axis_index("layer")
    feat = lax.axis_index("feat")
    core, zl = lax.rem(layer, 2), lax.div(layer, 2)
    zh = lax.rem(feat, 2)
    y = lax.rem(lax.div(feat, 2), 4)
    x = lax.div(feat, 8)

    def feat_of(xx, yy, zz):
        return (lax.rem(xx, 4) * 4 + lax.rem(yy, 4)) * 2 + zz

    def xy_dev(dx, dy):
        return {"layer": layer, "feat": feat_of(x + dx, y + dy, zh)}

    partner_z = {"layer": layer, "feat": feat_of(x, y, 1 - zh)}
    partner_c = {"layer": zl * 2 + 1 - core, "feat": feat}

    def z_dev(j):
        return {"layer": lax.rem(zl + j, 4) * 2 + core, "feat": feat}

    ids = Ids()
    pending = []

    def send(src, dst, name, dev):
        k = ids[name] if isinstance(name, (tuple, str)) else name
        copy = pltpu.make_async_remote_copy(
            src_ref=src, dst_ref=dst, send_sem=ssem.at[k], recv_sem=rsem.at[k],
            device_id=dev, device_id_type=MESH)
        copy.start()
        pending.append(copy)

    def recv(dst, name):
        k = ids[name] if isinstance(name, (tuple, str)) else name
        pltpu.make_async_remote_copy(
            src_ref=dst, dst_ref=dst, send_sem=ssem.at[k], recv_sem=rsem.at[k],
            device_id=partner_c, device_id_type=MESH).wait_recv()

    loads = {}

    def load(name, src, dst):
        loads[name] = pltpu.make_async_copy(src, dst, lsem.at[len(loads)])
        loads[name].start()

    for h in range(2):
        load(("e", h), encw_ref.at[:, pl.ds(h * HF, HF)], wenc.at[h, pl.ds(0, KD)])
    for h in range(2):
        load(("d", h), decw_ref.at[0, pl.ds(h * HF, HF)], w.at[h])

    barrier = pltpu.get_barrier_semaphore()
    peers = [xy_dev(dx, dy) for dx in range(4) for dy in range(4) if dx or dy]
    peers += [partner_z, partner_c] + [z_dev(j) for j in range(1, 4)]
    for dev in peers:
        pl.semaphore_signal(barrier, inc=1, device_id=dev, device_id_type=MESH)

    me = x * 4 + y
    zero = jnp.zeros((16, KP - KD), BF16)
    srcb[zh, me] = jnp.concatenate([src_ref[...], zero], axis=1)
    tg[zh] = tgt_ref[0]
    for h in range(2):
        wenc[h, pl.ds(KD, KP - KD)] = jnp.zeros((KP - KD, HF), BF16)
    pl.semaphore_wait(barrier, len(peers))

    for i in range(32):
        ids[("src", i)]
    send(srcb.at[zh, me], srcb.at[zh, me], zh * 16, partner_z)
    for dx in range(4):
        for dy in range(4):
            if dx or dy:
                send(srcb.at[zh, me], srcb.at[zh, me], zh * 16 + dx * 4 + dy, xy_dev(dx, dy))
    oz = 1 - zh
    recv(srcb.at[oz, me], oz * 16)
    for dx in range(4):
        for dy in range(4):
            if dx or dy:
                send(srcb.at[oz, me], srcb.at[oz, me], oz * 16 + dx * 4 + dy, xy_dev(dx, dy))
    send(tg.at[zh], tg.at[zh], "tgt", partner_z)

    def layer_sum_start(c, ph, half_of):
        xs[ph, c] = half_of(1 - core).astype(BF16)
        send(xs.at[ph, c], xr.at[ph, c], ("x", ph, c), partner_c)
        pown[c] = half_of(core)

    def layer_sum_z(c, ph):
        recv(xr.at[ph, c], ("x", ph, c))
        both = pown[c] + xr[ph, c].astype(F32)
        pown[c] = both
        zs[ph, c] = both.astype(BF16)
        for j in range(1, 4):
            to = lax.rem(zl + j, 4)
            send(zs.at[ph, c, pl.ds(to * 64, 64)], zr.at[ph, c, j - 1], ("z", ph, c, j), z_dev(j))

    def layer_sum_end(c, ph):
        total = pown[c, pl.ds(pl.multiple_of(zl * 64, 64), 64)]
        for j in range(1, 4):
            recv(zr.at[ph, c, j - 1], ("z", ph, c, j))
            total = total + zr[ph, c, j - 1].astype(F32)
        return total

    def share_start(c, ph, buf):
        mine = buf.at[c, core, zl]
        for j in range(1, 4):
            send(mine, mine, ("g", ph, c, j), z_dev(j))
        send(mine, mine, ("h", ph, c, 0), partner_c)

    def share_pass(c, ph, buf):
        for j in range(1, 4):
            at = buf.at[c, core, lax.rem(zl + 4 - j, 4)]
            recv(at, ("g", ph, c, j))
            send(at, at, ("h", ph, c, j), partner_c)

    def share_end(c, ph, buf):
        for j in range(4):
            recv(buf.at[c, 1 - core, lax.rem(zl + 4 - j, 4)], ("h", ph, c, j))

    def st_preact(c):
        for dx in range(4):
            for dy in range(4):
                if dx or dy:
                    p = lax.rem(x + 4 - dx, 4) * 4 + lax.rem(y + 4 - dy, 4)
                    recv(srcb.at[c, p], c * 16 + dx * 4 + dy)
        if c == 0:
            loads[("e", 0)].wait()
            loads[("e", 1)].wait()
        rows = srcb[c].reshape(CH, KP)
        layer_sum_start(c, 0, lambda h: dot(rows, wenc[h]))

    def st_preact_z(c):
        layer_sum_z(c, 0)

    def st_features(c):
        bias = bias_ref[pl.ds(core, 1), :]
        active = jnp.maximum(layer_sum_end(c, 0) + bias, 0.0)
        act[c] = active
        feats[c, core, zl] = (active * active).astype(BF16)
        share_start(c, 0, feats)

    def st_features_pass(c):
        share_pass(c, 0, feats)

    def axes(half):
        if half == 0:
            return x, y, (lambda da, db: xy_dev(da, db))
        return y, x, (lambda da, db: xy_dev(db, da))

    def sel(ref, half, c, a, b, nb):
        if half == 0:
            return ref.at[half, c, a, pl.ds(b, nb)]
        return ref.at[half, c, pl.ds(b, nb), a]

    def st_rebuilt(c):
        share_end(c, 0, feats)
        if c == 0:
            loads[("d", 0)].wait()
            loads[("d", 1)].wait()
        f0 = feats[c, 0].reshape(CH, HF)
        f1 = feats[c, 1].reshape(CH, HF)
        for half in range(2):
            for off, n in TILES:
                cols = pl.ds(half * HD + off, n)
                part = dot(f0, w[0, :, cols]) + dot(f1, w[1, :, cols])
                rb[half, c, :, :, :, pl.ds(off, n)] = part.astype(BF16).reshape(4, 4, 16, n)
            a, b, dev = axes(half)
            up, dn, op = lax.rem(a + 1, 4), lax.rem(a + 3, 4), lax.rem(a + 2, 4)
            send(sel(rb, half, c, op, 0, 2), t1.at[half, c, 0], ("r1", half, c, 0), dev(1, 0))
            send(sel(rb, half, c, op, 2, 2), t1.at[half, c, 1], ("r1", half, c, 1), dev(3, 0))
            send(sel(rb, half, c, up, 2, 2), t2.at[half, c, 0, pl.ds(2, 2)], ("r2", half, c, 0), dev(1, 0))
            send(sel(rb, half, c, dn, 0, 2), t2.at[half, c, 1, pl.ds(0, 2)], ("r2", half, c, 1), dev(3, 0))

    def st_transpose(c):
        for h in range(2):
            feat_t[h, :, pl.ds(c * CH, CH)] = feats[c, h].reshape(CH, HF).T

    def st_ring(c):
        for half in range(2):
            a, b, dev = axes(half)
            up, dn = lax.rem(a + 1, 4), lax.rem(a + 3, 4)
            recv(t1.at[half, c, 0], ("r1", half, c, 0))
            at = sel(rb, half, c, up, 0, 2)
            at[...] = (at[...].astype(F32) + t1[half, c, 0].astype(F32)).astype(BF16)
            send(at, t2.at[half, c, 0, pl.ds(0, 2)], ("r3", half, c, 0), dev(1, 0))
            recv(t1.at[half, c, 1], ("r1", half, c, 1))
            at = sel(rb, half, c, dn, 2, 2)
            at[...] = (at[...].astype(F32) + t1[half, c, 1].astype(F32)).astype(BF16)
            send(at, t2.at[half, c, 1, pl.ds(2, 2)], ("r3", half, c, 1), dev(3, 0))

    def st_second(c):
        for half in range(2):
            a, b, dev = axes(half)
            recv(t2.at[half, c, 0, pl.ds(2, 2)], ("r2", half, c, 0))
            recv(t2.at[half, c, 1, pl.ds(0, 2)], ("r2", half, c, 1))
            recv(t2.at[half, c, 0, pl.ds(0, 2)], ("r3", half, c, 0))
            recv(t2.at[half, c, 1, pl.ds(2, 2)], ("r3", half, c, 1))
            own = sel(rb, half, c, a, 0, 4)
            qs[half, c] = own[...].astype(F32) + t2[half, c, 0].astype(F32) + t2[half, c, 1].astype(F32)
            us[half, c] = qs[half, c].astype(BF16)
            for j in range(1, 4):
                send(us.at[half, c, lax.rem(b + j, 4)], qr.at[half, c, j - 1], ("q", half, c, j), dev(0, j))

    def st_swap(c):
        for half in range(2):
            a, b, dev = axes(half)
            total = qs[half, c, b]
            for j in range(1, 4):
                recv(qr.at[half, c, j - 1], ("q", half, c, j))
                total = total + qr[half, c, j - 1].astype(F32)
            us[half, c, b] = total.astype(BF16)
            send(us.at[half, c, b], ur.at[half, c], ("u", half, c), partner_z)

    def st_residual(c):
        if c == 0:
            recv(tg.at[oz], "tgt")
        for half in range(2):
            a, b, dev = axes(half)
            cols = pl.ds(half * HD, HD)
            recv(ur.at[half, c], ("u", half, c))
            total = us[half, c, b].astype(F32) + ur[half, c].astype(F32)
            total = total + dbias_ref[:, cols] - tg[c, :, cols].astype(F32)
            res[half, c, x, y] = total.astype(BF16)
            mine = res.at[half, c, x, y]
            for j in range(1, 4):
                send(mine, mine, ("a", half, c, j), dev(0, j))

    def st_gather(c):
        for half in range(2):
            a, b, dev = axes(half)
            for j in range(1, 4):
                at = (res.at[half, c, a, lax.rem(b + 4 - j, 4)] if half == 0
                      else res.at[half, c, lax.rem(b + 4 - j, 4), a])
                recv(at, ("a", half, c, j))
            lo, hi = sel(res, half, c, a, 0, 2), sel(res, half, c, a, 2, 2)
            send(lo, lo, ("b", half, c, 0), dev(1, 0))
            send(hi, hi, ("b", half, c, 1), dev(3, 0))
            send(hi, hi, ("b", half, c, 2), dev(1, 0))
            send(lo, lo, ("b", half, c, 3), dev(3, 0))

    def st_forward(c):
        for half in range(2):
            a, b, dev = axes(half)
            up, dn = lax.rem(a + 1, 4), lax.rem(a + 3, 4)
            at = sel(res, half, c, dn, 0, 2)
            recv(at, ("b", half, c, 0))
            send(at, at, ("f", half, c, 0), dev(1, 0))
            at = sel(res, half, c, up, 2, 2)
            recv(at, ("b", half, c, 1))
            send(at, at, ("f", half, c, 1), dev(3, 0))

    def st_summed(c):
        for half in range(2):
            a, b, dev = axes(half)
            up, dn, op = lax.rem(a + 1, 4), lax.rem(a + 3, 4), lax.rem(a + 2, 4)
            recv(sel(res, half, c, dn, 2, 2), ("b", half, c, 2))
            recv(sel(res, half, c, up, 0, 2), ("b", half, c, 3))
            recv(sel(res, half, c, op, 0, 2), ("f", half, c, 0))
            recv(sel(res, half, c, op, 2, 2), ("f", half, c, 1))

        def half_of(h):
            r0 = res[0, c].reshape(CH, HD)
            r1 = res[1, c].reshape(CH, HD)
            return jnp.concatenate(
                [dot_nt(r0, w[h, pl.ds(n, 256), pl.ds(0, HD)]) + dot_nt(r1, w[h, pl.ds(n, 256), pl.ds(HD, HD)])
                 for n in range(0, HF, 256)], axis=1)

        layer_sum_start(c, 1, half_of)

    def st_summed_z(c):
        layer_sum_z(c, 1)

    def st_fgrad(c):
        total = layer_sum_end(c, 1)
        fgr[c, core, zl] = (2.0 * act[c] * total).astype(BF16)
        share_start(c, 1, fgr)

    def st_fgrad_pass(c):
        share_pass(c, 1, fgr)

    def st_src_t(c):
        src_t[:, pl.ds(c * CH, CH)] = srcb[c].reshape(CH, KP).T

    def st_enc_grad(c):
        share_end(c, 1, fgr)
        lhs = src_t[:, pl.ds(c * CH, CH)]
        for h in range(2):
            part = dot(lhs, fgr[c, h].reshape(CH, HF))
            if c == 0:
                egacc[h] = part
            else:
                egout[:, pl.ds(h * HF, HF)] = (egacc[h] + part)[:KD].astype(BF16)

    outs = []

    def st_dec_grad(_):
        for h in range(2):
            for m in range(0, HF, 256):
                lhs = feat_t[h, pl.ds(m, 256), :]
                for half in range(2):
                    for off, n in TILES:
                        rhs = res[half, :, :, :, :, pl.ds(off, n)].reshape(2 * CH, n)
                        stag[pl.ds(h * HF + m, 256), pl.ds(half * HD + off, n)] = dot(lhs, rhs).astype(BF16)
                rows = pl.ds(h * HF + m, 256)
                copy = pltpu.make_async_copy(stag.at[rows], dg_ref.at[0, rows], lsem.at[4 + len(outs)])
                copy.start()
                outs.append(copy)

    order = [
        (st_preact, 0), (st_preact, 1), (st_preact_z, 0), (st_preact_z, 1), (st_features, 0), (st_features, 1),
        (st_features_pass, 0), (st_features_pass, 1), (st_rebuilt, 0), (st_rebuilt, 1), (st_transpose, 0), (st_ring, 0),
        (st_second, 0), (st_ring, 1), (st_swap, 0), (st_second, 1), (st_transpose, 1), (st_residual, 0), (st_swap, 1),
        (st_src_t, 0), (st_src_t, 1), (st_gather, 0), (st_residual, 1), (st_forward, 0), (st_gather, 1),
        (st_summed, 0), (st_forward, 1), (st_summed_z, 0), (st_summed, 1), (st_fgrad, 0), (st_summed_z, 1),
        (st_fgrad_pass, 0), (st_dec_grad, 0), (st_fgrad, 1), (st_enc_grad, 0), (st_fgrad_pass, 1), (st_enc_grad, 1),
    ]
    for stage, c in order:
        stage(c)
    copy = pltpu.make_async_copy(egout, eg_ref, lsem.at[4 + len(outs)])
    copy.start()
    outs.append(copy)
    for copy in pending:
        copy.wait_send()
    for copy in outs:
        copy.wait()
    assert len(ids.table) <= N_SEM


def step(source, enc_weight, enc_bias, dec_weight, dec_bias, targets):
    vmem = pl.BlockSpec(memory_space=pltpu.VMEM)
    hbm = pl.BlockSpec(memory_space=pl.ANY)
    V = pltpu.VMEM
    return pl.pallas_call(
        kernel,
        out_shape=(
            jax.ShapeDtypeStruct((KD, NF), BF16),
            jax.ShapeDtypeStruct((1, NF, D), BF16),
        ),
        in_specs=[vmem, hbm, vmem, hbm, vmem, vmem],
        out_specs=(hbm, hbm),
        scratch_shapes=[
            V((2, 16, 16, KP), BF16),
            V((2, KP, HF), BF16),
            V((2, HF, D), BF16),
            V((2, 16, D), BF16),
            V((2, CH, HF), F32),
            V((2, 2, CH, HF), BF16),
            V((2, 2, CH, HF), BF16),
            V((2, 2, CH, HF), BF16),
            V((2, 2, 3, 64, HF), BF16),
            V((2, 64, HF), F32),
            V((2, 2, 4, 64, HF), BF16),
            V((2, HF, 2 * CH), BF16),
            V((KP, 2 * CH), BF16),
            V((2, 2, 4, 64, HF), BF16),
            V((2, KP, HF), F32),
            V((2, 2, 4, 4, 16, HD), BF16),
            V((2, 2, 2, 2, 16, HD), BF16),
            V((2, 2, 2, 4, 16, HD), BF16),
            V((2, 2, 4, 16, HD), F32),
            V((2, 2, 3, 16, HD), BF16),
            V((2, 2, 4, 16, HD), BF16),
            V((2, 2, 16, HD), BF16),
            V((2, 2, 4, 4, 16, HD), BF16),
            V((NF, D), BF16),
            V((KD, NF), BF16),
            pltpu.SemaphoreType.DMA((N_SEM,)),
            pltpu.SemaphoreType.DMA((N_SEM,)),
            pltpu.SemaphoreType.DMA((16,)),
        ],
        compiler_params=pltpu.CompilerParams(
            collective_id=0, has_side_effects=True, vmem_limit_bytes=60 * 1024 * 1024),
    )(source, enc_weight, enc_bias.reshape(2, HF), dec_weight, dec_bias, targets)


def solution(mesh):
    placed = (
        P("feat", "layer"),
        P("layer", "feat"),
        P("feat"),
        P("layer", "feat", None),
        P("layer", None),
        P("layer", "feat", None),
    )
    return jax.shard_map(
        step,
        mesh=mesh,
        in_specs=placed,
        out_specs=(P("layer", "feat"), P("layer", "feat", None)),
        check_vma=False,
    )
```

```python
import math

import jax
import jax.numpy as jnp
from jax import lax
from jax.experimental import pallas as pl
from jax.experimental.pallas import tpu as pltpu
from jax.sharding import PartitionSpec as P

MESH = pl.DeviceIdType.MESH
F32 = jnp.float32
BF16 = jnp.bfloat16

D = 2304
HD = D // 2
NF = 1024
HF = NF // 2
KD = 288
KP = 384
CH = 256
TILES = ((0, 256), (256, 256), (512, 256), (768, 256), (1024, 128))


def dot(a, b):
    return jnp.dot(a, b, preferred_element_type=F32)


def dot_nt(a, b):
    return lax.dot_general(a, b, (((1,), (1,)), ((), ())), preferred_element_type=F32)


class Ids:
    def __init__(self):
        self.table = {}

    def __getitem__(self, name):
        return self.table.setdefault(name, len(self.table))


N_RECV = 96
N_SEND = 31


def kernel(src_hbm, encw_ref, bias_hbm, decw_ref, dbias_hbm, tgt_hbm, eg_ref, dg_ref,
           src_ref, bias_ref, dbias_ref,
           srcb, wenc, w, tg, pown, acc, xs, xr, ls, nb, fb, act, feats, feat_t, src_t, fgr, egacc,
           rb, t1, t2, qs, qr, us, ur, res, rl, stag, egout, ssem, rsem, lsem):
    layer = lax.axis_index("layer")
    feat = lax.axis_index("feat")
    core, zl = lax.rem(layer, 2), lax.div(layer, 2)
    zh = lax.rem(feat, 2)
    y = lax.rem(lax.div(feat, 2), 4)
    x = lax.div(feat, 8)

    def feat_of(xx, yy, zz):
        return (lax.rem(xx, 4) * 4 + lax.rem(yy, 4)) * 2 + zz

    def xy_dev(dx, dy):
        return {"layer": layer, "feat": feat_of(x + dx, y + dy, zh)}

    partner_z = {"layer": layer, "feat": feat_of(x, y, 1 - zh)}
    partner_c = {"layer": zl * 2 + 1 - core, "feat": feat}

    def ring_dev(d):
        z = lax.rem(zh * 4 + zl + 8 + d, 8)
        return {"layer": lax.rem(z, 4) * 2 + core, "feat": feat_of(x, y, lax.div(z, 4))}

    ids, sids = Ids(), Ids()
    tiles, stage_tiles, now = {}, {}, ["start"]

    def bulk(n):
        wide = max(k for k in range(1, 19) if n % k == 0 and n // k <= 32)
        return w.at[0, pl.ds(0, n // wide * 16), pl.ds(0, wide * 128)]

    def count(ref):
        return math.prod(ref.shape) // 2048

    def send(src, dst, name, dev, slot=0, batch=None, tally=True):
        batch = batch or now[0]
        stage_tiles[batch] = stage_tiles.get(batch, 0) + count(src)
        if tally:
            tiles[name] = tiles.get(name, 0) + count(src)
        pltpu.make_async_remote_copy(
            src_ref=src, dst_ref=dst, send_sem=ssem.at[sids[batch]], recv_sem=rsem.at[ids[name] + slot],
            device_id=dev, device_id_type=MESH).start()

    def recv(name, slot=0, dst=None):
        if dst is None:
            dst = bulk(tiles[name])
        pltpu.make_async_copy(dst, dst, rsem.at[ids[name] + slot]).wait()

    loads = {}

    def load(name, src, dst):
        loads[name] = pltpu.make_async_copy(src, dst, lsem.at[len(loads)])
        loads[name].start()

    load("src", src_hbm, src_ref)
    load("tgt", tgt_hbm.at[0], tg.at[zh])
    load("bias", bias_hbm, bias_ref)
    load("dbias", dbias_hbm, dbias_ref)
    for h in range(2):
        load(("e", h), encw_ref.at[:, pl.ds(h * HF, HF)], wenc.at[h, pl.ds(0, KD)])
    for h in range(2):
        load(("d", h), decw_ref.at[0, pl.ds(h * HF, HF)], w.at[h])

    barrier = pltpu.get_barrier_semaphore()
    peers = [xy_dev(dx, dy) for dx in range(4) for dy in range(4) if dx or dy]
    peers += [partner_z, partner_c] + [ring_dev(d) for d in (1, -1, 3, -3)]
    for dev in peers:
        pl.semaphore_signal(barrier, inc=1, device_id=dev, device_id_type=MESH)

    me = x * 4 + y
    zero = jnp.zeros((16, KP - KD), BF16)
    loads['src'].wait()
    srcb[zh, me] = jnp.concatenate([src_ref[...], zero], axis=1)
    for h in range(2):
        wenc[h, pl.ds(KD, KP - KD)] = jnp.zeros((KP - KD, HF), BF16)
    pl.semaphore_wait(barrier, len(peers))

    for i in range(2):
        ids[("src", i)]
    oz = 1 - zh
    send(srcb.at[zh, me], srcb.at[zh, me], "srcz", partner_z)

    def spread(z, batch):
        for dx in range(4):
            for dy in range(4):
                if dx or dy:
                    send(srcb.at[z, me], srcb.at[z, me], ("src", 0), xy_dev(dx, dy), z, batch=batch)

    @pl.when(zh == 0)
    def _():
        spread(zh, "own")

    recv("srcz")
    now[0] = "relay"
    spread(oz, "relay")

    @pl.when(zh == 1)
    def _():
        spread(zh, "own")

    tiles[("src", 0)] //= 3
    stage_tiles["own"] //= 2
    for name in ("tgt", "bias", "dbias"):
        loads[name].wait()
    send(tg.at[zh], tg.at[zh], "tgt", partner_z)

    is_end = (zl == 0) | (zl == 3)
    is_inner = (zl == 1) | (zl == 2)
    toward = 1 - 2 * lax.div(zl, 2)
    far_dev = {"layer": lax.rem(zl + toward + 4, 4) * 2 + core, "feat": feat}
    near_dev = {"layer": lax.rem(zl - toward + 4, 4) * 2 + core, "feat": feat}

    def layer_sum_start(c, ph, half_of):
        xs[ph, c] = half_of(1 - core).astype(BF16)
        for b in range(4):
            rows = pl.ds(b * 64, 64)
            send(xs.at[ph, c, rows], xr.at[ph, c, rows], ("x", ph, c, b), partner_c)
        pown[c] = half_of(core)

    def line_start(c, ph, b):
        rows = pl.ds(b * 64, 64)
        recv(("x", ph, c, b))
        own = pown[c, rows] + xr[ph, c, rows].astype(F32)
        pown[c, rows] = own
        acc[c, rows] = own
        ids[("n", ph, c, b)], ids[("f", ph, c, b)]

        @pl.when(is_end)
        def _():
            ls[0, ph, c, rows] = own.astype(BF16)
            send(ls.at[0, ph, c, rows], nb.at[ph, c, rows], ("n", ph, c, b), far_dev, batch=("end", ph, c))

    def line_near(c, ph, b):
        rows = pl.ds(b * 64, 64)

        @pl.when(is_inner)
        def _():
            recv(("n", ph, c, b), dst=nb.at[ph, c, rows])
            both = acc[c, rows] + nb[ph, c, rows].astype(F32)
            acc[c, rows] = both
            ls[0, ph, c, rows] = both.astype(BF16)
            send(ls.at[0, ph, c, rows], fb.at[ph, c, rows], ("f", ph, c, b), far_dev, batch=("inner", ph, c))

    def line_far(c, ph, b, inner):
        rows = pl.ds(b * 64, 64)
        batch = ("inner" if inner else "end", ph, c)

        @pl.when(is_inner if inner else is_end)
        def _():
            recv(("f", ph, c, b), dst=fb.at[ph, c, rows])
            beyond = fb[ph, c, rows].astype(F32)
            if inner:
                ls[1, ph, c, rows] = (pown[c, rows] + beyond).astype(BF16)
                send(ls.at[1, ph, c, rows], fb.at[ph, c, rows], ("f", ph, c, b), near_dev, batch=batch)
            total = acc[c, rows] + beyond
            if ph == 0:
                bias = bias_ref[:, pl.ds(pl.multiple_of(core * HF, HF), HF)]
                active = jnp.maximum(total + bias, 0.0)
                act[c, rows] = active
                feats[c, core, b] = (active * active).astype(BF16)
                mine = feats.at[c, core, b]
            else:
                fgr[c, core, b] = (2.0 * act[c, rows] * total).astype(BF16)
                mine = fgr.at[c, core, b]
            send(mine, mine, ("h", ph, c), partner_c, batch=batch, tally=inner)

    def st_preact(c):
        recv(("src", 0), c)
        if c == 0:
            loads[("e", 0)].wait()
            loads[("e", 1)].wait()
        rows = srcb[c].reshape(CH, KP)
        layer_sum_start(c, 0, lambda h: dot(rows, wenc[h]))

    def st_line(c, ph, b):
        line_start(c, ph, b)

    def st_near(c, ph, b):
        line_near(c, ph, b)

    def st_far(c, ph, b):
        line_far(c, ph, b, True)

    def st_far_end(c, ph, b):
        line_far(c, ph, b, False)

    def axes(half):
        if half == 0:
            return x, y, (lambda da, db: xy_dev(da, db))
        return y, x, (lambda da, db: xy_dev(db, da))

    def sel(ref, half, c, a, b, nb):
        if half == 0:
            return ref.at[half, c, a, pl.ds(b, nb)]
        return ref.at[half, c, pl.ds(b, nb), a]

    def st_rebuilt(c):
        recv(("h", 0, c))
        if c == 0:
            loads[("d", 0)].wait()
            loads[("d", 1)].wait()
        f0 = feats[c, 0].reshape(CH, HF)
        f1 = feats[c, 1].reshape(CH, HF)
        for half in range(2):
            for off, n in TILES:
                cols = pl.ds(half * HD + off, n)
                part = dot(f0, w[0, :, cols]) + dot(f1, w[1, :, cols])
                rb[half, c, :, :, :, pl.ds(off, n)] = part.astype(BF16).reshape(4, 4, 16, n)
            a, b, dev = axes(half)
            up, dn, op = lax.rem(a + 1, 4), lax.rem(a + 3, 4), lax.rem(a + 2, 4)
            send(sel(rb, half, c, op, 0, 2), t1.at[half, c, 0], ("r1", half, c, 0), dev(1, 0))
            send(sel(rb, half, c, op, 2, 2), t1.at[half, c, 1], ("r1", half, c, 1), dev(3, 0))
            send(sel(rb, half, c, up, 2, 2), t2.at[half, c, 0, pl.ds(2, 2)], ("t2", half, c), dev(1, 0))
            send(sel(rb, half, c, dn, 0, 2), t2.at[half, c, 1, pl.ds(0, 2)], ("t2", half, c), dev(3, 0))

    def st_transpose(c):
        for h in range(2):
            feat_t[h, :, pl.ds(c * CH, CH)] = feats[c, h].reshape(CH, HF).T

    def st_ring(c):
        for half in range(2):
            a, b, dev = axes(half)
            up, dn = lax.rem(a + 1, 4), lax.rem(a + 3, 4)
            recv(("r1", half, c, 0))
            at = sel(rb, half, c, up, 0, 2)
            at[...] = (at[...].astype(F32) + t1[half, c, 0].astype(F32)).astype(BF16)
            send(at, t2.at[half, c, 0, pl.ds(0, 2)], ("t2", half, c), dev(1, 0))
            recv(("r1", half, c, 1))
            at = sel(rb, half, c, dn, 2, 2)
            at[...] = (at[...].astype(F32) + t1[half, c, 1].astype(F32)).astype(BF16)
            send(at, t2.at[half, c, 1, pl.ds(2, 2)], ("t2", half, c), dev(3, 0))

    def st_second(c):
        for half in range(2):
            a, b, dev = axes(half)
            recv(("t2", half, c))
            own = sel(rb, half, c, a, 0, 4)
            qs[half, c] = own[...].astype(F32) + t2[half, c, 0].astype(F32) + t2[half, c, 1].astype(F32)
            us[half, c] = qs[half, c].astype(BF16)
            for j in range(1, 4):
                send(us.at[half, c, lax.rem(b + j, 4)], qr.at[half, c, j - 1], ("q", half, c), dev(0, j))

    def st_swap(c):
        for half in range(2):
            a, b, dev = axes(half)
            total = qs[half, c, b]
            recv(("q", half, c))
            for j in range(1, 4):
                total = total + qr[half, c, j - 1].astype(F32)
            us[half, c, b] = total.astype(BF16)
            send(us.at[half, c, b], rl.at[half, c], ("v", half, c), ring_dev(1 - 2 * half))

    def st_swap_pass(c):
        for half in range(2):
            recv(("v", half, c))
            send(rl.at[half, c], ur.at[half, c], ("u", half, c), ring_dev(3 - 6 * half))

    def st_residual(c):
        if c == 0:
            recv("tgt")
        for half in range(2):
            a, b, dev = axes(half)
            cols = pl.ds(half * HD, HD)
            recv(("u", half, c))
            total = us[half, c, b].astype(F32) + ur[half, c].astype(F32)
            total = total + dbias_ref[:, cols] - tg[c, :, cols].astype(F32)
            res[half, c, x, y] = total.astype(BF16)
            mine = res.at[half, c, x, y]
            for j in range(1, 4):
                send(mine, mine, ("a", half, c), dev(0, j))

    def st_gather(c):
        for half in range(2):
            a, b, dev = axes(half)
            recv(("a", half, c))
            lo, hi = sel(res, half, c, a, 0, 2), sel(res, half, c, a, 2, 2)
            send(lo, lo, ("b", half, c, 0), dev(1, 0))
            send(hi, hi, ("b", half, c, 1), dev(3, 0))
            send(hi, hi, ("e", half, c), dev(1, 0))
            send(lo, lo, ("e", half, c), dev(3, 0))

    def st_forward(c):
        for half in range(2):
            a, b, dev = axes(half)
            up, dn = lax.rem(a + 1, 4), lax.rem(a + 3, 4)
            at = sel(res, half, c, dn, 0, 2)
            recv(("b", half, c, 0))
            send(at, at, ("e", half, c), dev(1, 0))
            at = sel(res, half, c, up, 2, 2)
            recv(("b", half, c, 1))
            send(at, at, ("e", half, c), dev(3, 0))

    def st_summed(c):
        for half in range(2):
            recv(("e", half, c))

        def half_of(h):
            r0 = res[0, c].reshape(CH, HD)
            r1 = res[1, c].reshape(CH, HD)
            return jnp.concatenate(
                [dot_nt(r0, w[h, pl.ds(n, 256), pl.ds(0, HD)]) + dot_nt(r1, w[h, pl.ds(n, 256), pl.ds(HD, HD)])
                 for n in range(0, HF, 256)], axis=1)

        layer_sum_start(c, 1, half_of)

    def st_src_t(c):
        src_t[:, pl.ds(c * CH, CH)] = srcb[c].reshape(CH, KP).T

    def st_enc_grad(c):
        recv(("h", 1, c))
        lhs = src_t[:, pl.ds(c * CH, CH)]
        for h in range(2):
            part = dot(lhs, fgr[c, h].reshape(CH, HF))
            if c == 0:
                egacc[h] = part
            else:
                egout[:, pl.ds(h * HF, HF)] = (egacc[h] + part)[:KD].astype(BF16)

    outs = []

    def put(src, dst):
        outs.append(pltpu.make_async_copy(src, dst, lsem.at[8 + len(outs)]))
        outs[-1].start()

    def st_dec_grad(h):
        for m in range(0, HF, 256):
            lhs = feat_t[h, pl.ds(m, 256), :]
            for half in range(2):
                for off, n in TILES:
                    rhs = res[half, :, :, :, :, pl.ds(off, n)].reshape(2 * CH, n)
                    stag[pl.ds(h * HF + m, 256), pl.ds(half * HD + off, n)] = dot(lhs, rhs).astype(BF16)
            rows = pl.ds(h * HF + m, 256)
            put(stag.at[rows], dg_ref.at[0, rows])

    def line(c, ph):
        return [(st_line, c, ph, b) for b in range(4)]

    def near(c, ph, *bs):
        return [(st_near, c, ph, b) for b in bs]

    def far(c, ph, *bs):
        return [(st_far, c, ph, b) for b in bs]

    def end(c, ph):
        return [(st_far_end, c, ph, b) for b in range(4)]

    order = [
        (st_preact, 0), *line(0, 0), (st_preact, 1), *line(1, 0),
        *near(0, 0, 0, 1, 2), *far(0, 0, 0), *near(0, 0, 3), *far(0, 0, 1), *near(1, 0, 0), *far(0, 0, 2),
        *near(1, 0, 1), *far(0, 0, 3), *near(1, 0, 2, 3), *end(0, 0),
        (st_rebuilt, 0), *far(1, 0, 0, 1, 2, 3), *end(1, 0), (st_ring, 0), (st_transpose, 0), (st_src_t, 0), (st_src_t, 1),
        (st_second, 0), (st_rebuilt, 1), (st_swap, 0), (st_transpose, 1), (st_ring, 1), (st_swap_pass, 0), (st_second, 1),
        (st_residual, 0), (st_swap, 1), (st_gather, 0), (st_swap_pass, 1), (st_forward, 0), (st_residual, 1),
        (st_summed, 0), *line(0, 1), (st_gather, 1),
        *near(0, 1, 0, 1), (st_forward, 1), *near(0, 1, 2), *far(0, 1, 0), *near(0, 1, 3), *far(0, 1, 1, 2, 3),
        (st_summed, 1), *line(1, 1), *end(0, 1), (st_dec_grad, 0),
        *near(1, 1, 0, 1, 2), *far(1, 1, 0), *near(1, 1, 3), *far(1, 1, 1, 2, 3),
        (st_dec_grad, 1), (st_enc_grad, 0), *end(1, 1), (st_enc_grad, 1),
    ]
    for stage, *args in order:
        now[0] = (stage.__name__, *args)
        stage(*args)
    put(egout, eg_ref)
    for batch, n in stage_tiles.items():
        if batch[0] in ("end", "inner"):
            @pl.when(is_end if batch[0] == "end" else is_inner)
            def _():
                pltpu.make_async_copy(bulk(n), bulk(n), ssem.at[sids[batch]]).wait()
        else:
            pltpu.make_async_copy(bulk(n), bulk(n), ssem.at[sids[batch]]).wait()
    for copy in outs:
        copy.wait()
    assert len(ids.table) == N_RECV and len(sids.table) == N_SEND, (len(ids.table), len(sids.table))


def step(source, enc_weight, enc_bias, dec_weight, dec_bias, targets):
    vmem = pl.BlockSpec(memory_space=pltpu.VMEM)
    hbm = pl.BlockSpec(memory_space=pltpu.HBM)
    V = pltpu.VMEM
    return pl.pallas_call(
        kernel,
        out_shape=(
            jax.ShapeDtypeStruct((KD, NF), BF16),
            jax.ShapeDtypeStruct((1, NF, D), BF16),
        ),
        in_specs=[hbm] * 6,
        out_specs=(pl.BlockSpec(memory_space=pl.ANY),) * 2,
        scratch_shapes=[
            V((16, KD), BF16),
            V((1, NF), F32),
            V((1, D), F32),
            V((2, 16, 16, KP), BF16),
            V((2, KP, HF), BF16),
            V((2, HF, D), BF16),
            V((2, 16, D), BF16),
            V((2, CH, HF), F32),
            V((2, CH, HF), F32),
            V((2, 2, CH, HF), BF16),
            V((2, 2, CH, HF), BF16),
            V((2, 2, 2, CH, HF), BF16),
            V((2, 2, CH, HF), BF16),
            V((2, 2, CH, HF), BF16),
            V((2, CH, HF), F32),
            V((2, 2, 4, 64, HF), BF16),
            V((2, HF, 2 * CH), BF16),
            V((KP, 2 * CH), BF16),
            V((2, 2, 4, 64, HF), BF16),
            V((2, KP, HF), F32),
            V((2, 2, 4, 4, 16, HD), BF16),
            V((2, 2, 2, 2, 16, HD), BF16),
            V((2, 2, 2, 4, 16, HD), BF16),
            V((2, 2, 4, 16, HD), F32),
            V((2, 2, 3, 16, HD), BF16),
            V((2, 2, 4, 16, HD), BF16),
            V((2, 2, 16, HD), BF16),
            V((2, 2, 4, 4, 16, HD), BF16),
            V((2, 2, 16, HD), BF16),
            V((NF, D), BF16),
            V((KD, NF), BF16),
            pltpu.SemaphoreType.DMA((N_SEND,)),
            pltpu.SemaphoreType.DMA((N_RECV,)),
            pltpu.SemaphoreType.DMA((13,)),
        ],
        compiler_params=pltpu.CompilerParams(
            collective_id=0, has_side_effects=True, vmem_limit_bytes=48 * 1024 * 1024),
    )(*[pltpu.with_memory_space_constraint(a, pltpu.HBM)
        for a in (source, enc_weight, enc_bias.reshape(1, NF), dec_weight, dec_bias, targets)])


def solution(mesh):
    placed = (
        P("feat", "layer"),
        P("layer", "feat"),
        P("feat"),
        P("layer", "feat", None),
        P("layer", None),
        P("layer", "feat", None),
    )
    return jax.shard_map(
        step,
        mesh=mesh,
        in_specs=placed,
        out_specs=(P("layer", "feat"), P("layer", "feat", None)),
        check_vma=False,
    )
```

```python
import math

import jax
import jax.numpy as jnp
from jax import lax
from jax.experimental import pallas as pl
from jax.experimental.pallas import tpu as pltpu
from jax.sharding import PartitionSpec as P

MESH = pl.DeviceIdType.MESH
F32 = jnp.float32
BF16 = jnp.bfloat16

D = 2304
HD = D // 2
NF = 1024
HF = NF // 2
KD = 288
KP = 384
CH = 256
GW = 384
NG = HD // GW
NB = 8
RB = CH // NB
TILES = ((0, 256), (256, 256), (512, 256), (768, 256), (1024, 128))


def dot(a, b):
    return jnp.dot(a, b, preferred_element_type=F32)


def dot_nt(a, b):
    return lax.dot_general(a, b, (((1,), (1,)), ((), ())), preferred_element_type=F32)


class Ids:
    def __init__(self):
        self.table = {}

    def __getitem__(self, name):
        return self.table.setdefault(name, len(self.table))


N_RECV = 122
N_SEND = 29


def kernel(src_hbm, encw_ref, bias_hbm, decw_ref, dbias_hbm, tgt_hbm, eg_ref, dg_ref,
           src_ref, bias_ref, dbias_ref,
           srcb, wenc, w, tg, pown, acc, xacc, xs, xr, ls, nb, fb, act, feats, feat_t, src_t, fgr, egacc,
           rb, t1, t2, qs, qr, us, ur, res, rl, stag, egout, ssem, rsem, lsem):
    layer = lax.axis_index("layer")
    feat = lax.axis_index("feat")
    core, zl = lax.rem(layer, 2), lax.div(layer, 2)
    zh = lax.rem(feat, 2)
    y = lax.rem(lax.div(feat, 2), 4)
    x = lax.div(feat, 8)

    def feat_of(xx, yy, zz):
        return (lax.rem(xx, 4) * 4 + lax.rem(yy, 4)) * 2 + zz

    def xy_dev(dx, dy):
        return {"layer": layer, "feat": feat_of(x + dx, y + dy, zh)}

    partner_z = {"layer": layer, "feat": feat_of(x, y, 1 - zh)}
    partner_c = {"layer": zl * 2 + 1 - core, "feat": feat}

    def ring_dev(d):
        z = lax.rem(zh * 4 + zl + 8 + d, 8)
        return {"layer": lax.rem(z, 4) * 2 + core, "feat": feat_of(x, y, lax.div(z, 4))}

    ids, sids = Ids(), Ids()
    tiles, stage_tiles, now = {}, {}, ["start"]

    def bulk(n):
        wide = max(k for k in range(1, 19) if n % k == 0 and n // k <= 32)
        return w.at[0, pl.ds(0, n // wide * 16), pl.ds(0, wide * 128)]

    def count(ref):
        return math.prod(ref.shape) // 2048

    def send(src, dst, name, dev, slot=0, batch=None, tally=True):
        batch = batch or now[0]
        stage_tiles[batch] = stage_tiles.get(batch, 0) + count(src)
        if tally:
            tiles[name] = tiles.get(name, 0) + count(src)
        pltpu.make_async_remote_copy(
            src_ref=src, dst_ref=dst, send_sem=ssem.at[sids[batch]], recv_sem=rsem.at[ids[name] + slot],
            device_id=dev, device_id_type=MESH).start()

    def recv(name, slot=0, dst=None):
        if dst is None:
            dst = bulk(tiles[name])
        pltpu.make_async_copy(dst, dst, rsem.at[ids[name] + slot]).wait()

    loads = {}

    def load(name, src, dst):
        loads[name] = pltpu.make_async_copy(src, dst, lsem.at[len(loads)])
        loads[name].start()

    load("src", src_hbm, src_ref)
    load("tgt", tgt_hbm.at[0], tg.at[zh])
    load("bias", bias_hbm, bias_ref)
    load("dbias", dbias_hbm, dbias_ref)
    for h in range(2):
        load(("e", h), encw_ref.at[:, pl.ds(h * HF, HF)], wenc.at[h, pl.ds(0, KD)])
    for h in range(2):
        load(("d", h), decw_ref.at[0, pl.ds(h * HF, HF)], w.at[h])

    barrier = pltpu.get_barrier_semaphore()
    peers = [xy_dev(dx, dy) for dx in range(4) for dy in range(4) if dx or dy]
    peers += [partner_z, partner_c] + [ring_dev(d) for d in (1, -1, 3, -3)]
    for dev in peers:
        pl.semaphore_signal(barrier, inc=1, device_id=dev, device_id_type=MESH)

    me = x * 4 + y
    zero = jnp.zeros((16, KP - KD), BF16)
    loads['src'].wait()
    srcb[zh, me] = jnp.concatenate([src_ref[...], zero], axis=1)
    for h in range(2):
        wenc[h, pl.ds(KD, KP - KD)] = jnp.zeros((KP - KD, HF), BF16)
    pl.semaphore_wait(barrier, len(peers))

    for i in range(2):
        ids[("src", i)]
    oz = 1 - zh
    send(srcb.at[zh, me], srcb.at[zh, me], "srcz", partner_z)

    def spread(z, batch):
        for dx in range(4):
            for dy in range(4):
                if dx or dy:
                    send(srcb.at[z, me], srcb.at[z, me], ("src", 0), xy_dev(dx, dy), z, batch=batch)

    @pl.when(zh == 0)
    def _():
        spread(zh, "own")

    recv("srcz")
    now[0] = "relay"
    spread(oz, "relay")

    @pl.when(zh == 1)
    def _():
        spread(zh, "own")

    tiles[("src", 0)] //= 3
    stage_tiles["own"] //= 2
    for name in ("tgt", "bias", "dbias"):
        loads[name].wait()
    send(tg.at[zh], tg.at[zh], "tgt", partner_z)

    is_end = (zl == 0) | (zl == 3)
    is_inner = (zl == 1) | (zl == 2)
    toward = 1 - 2 * lax.div(zl, 2)
    far_dev = {"layer": lax.rem(zl + toward + 4, 4) * 2 + core, "feat": feat}
    near_dev = {"layer": lax.rem(zl - toward + 4, 4) * 2 + core, "feat": feat}

    def share_x(c, ph):
        for b in range(2):
            rows = pl.ds(b * 128, 128)
            send(xs.at[ph, c, rows], xr.at[ph, c, rows], ("x", ph, c, b), partner_c)

    def layer_sum_start(c, ph, half_of):
        xs[ph, c] = half_of(1 - core).astype(BF16)
        share_x(c, ph)
        pown[c] = half_of(core)

    def line_start(c, ph, b):
        rows = pl.ds(b * RB, RB)
        if b % (NB // 2) == 0:
            recv(("x", ph, c, b // (NB // 2)))
        own = pown[c, rows] + xr[ph, c, rows].astype(F32)
        pown[c, rows] = own
        acc[c, rows] = own
        ids[("n", ph, c, b)], ids[("f", ph, c, b)]

        @pl.when(is_end)
        def _():
            ls[0, ph, c, rows] = own.astype(BF16)
            send(ls.at[0, ph, c, rows], nb.at[ph, c, rows], ("n", ph, c, b), far_dev, batch=("end", ph, c))

    def line_near(c, ph, b):
        rows = pl.ds(b * RB, RB)

        @pl.when(is_inner)
        def _():
            recv(("n", ph, c, b), dst=nb.at[ph, c, rows])
            both = acc[c, rows] + nb[ph, c, rows].astype(F32)
            acc[c, rows] = both
            ls[0, ph, c, rows] = both.astype(BF16)
            send(ls.at[0, ph, c, rows], fb.at[ph, c, rows], ("f", ph, c, b), far_dev, batch=("inner", ph, c))

    def line_far(c, ph, b, inner):
        rows = pl.ds(b * RB, RB)
        batch = ("inner" if inner else "end", ph, c)

        @pl.when(is_inner if inner else is_end)
        def _():
            recv(("f", ph, c, b), dst=fb.at[ph, c, rows])
            beyond = fb[ph, c, rows].astype(F32)
            if inner:
                ls[1, ph, c, rows] = (pown[c, rows] + beyond).astype(BF16)
                send(ls.at[1, ph, c, rows], fb.at[ph, c, rows], ("f", ph, c, b), near_dev, batch=batch)
            total = acc[c, rows] + beyond
            if ph == 0:
                bias = bias_ref[:, pl.ds(pl.multiple_of(core * HF, HF), HF)]
                active = jnp.maximum(total + bias, 0.0)
                act[c, rows] = active
                feats[c, core, b] = (active * active).astype(BF16)
                mine = feats.at[c, core, b]
            else:
                fgr[c, core, b] = (2.0 * act[c, rows] * total).astype(BF16)
                mine = fgr.at[c, core, b]
            send(mine, mine, ("h", ph, c), partner_c, batch=batch, tally=inner)

    def st_preact(k):
        recv(("src", 0), k)
        if k == 0:
            loads[("e", 0)].wait()
            loads[("e", 1)].wait()
        rows = srcb[k].reshape(CH, KP)
        layer_sum_start(k, 0, lambda h: dot(rows, wenc[h]))

    def st_line(c, ph, b):
        line_start(c, ph, b)

    def st_near(c, ph, b):
        line_near(c, ph, b)

    def st_far(c, ph, b):
        line_far(c, ph, b, True)

    def st_far_end(c, ph, b):
        line_far(c, ph, b, False)

    def axes(half):
        if half == 0:
            return x, y, (lambda da, db: xy_dev(da, db))
        return y, x, (lambda da, db: xy_dev(db, da))

    def sel(ref, half, c, a, b, nb, cols):
        if half == 0:
            return ref.at[half, c, a, pl.ds(b, nb), :, cols]
        return ref.at[half, c, pl.ds(b, nb), a, :, cols]

    def group(g):
        return pl.ds(g * GW, GW)

    def st_rebuilt(c, g):
        if g == 0:
            recv(("h", 0, c))
        if g == 0 and c == 0:
            loads[("d", 0)].wait()
            loads[("d", 1)].wait()
        f0 = feats[c, 0].reshape(CH, HF)
        f1 = feats[c, 1].reshape(CH, HF)
        cg = group(g)
        for half in range(2):
            for off, n in ((0, 256), (256, 128)):
                off = g * GW + off
                cols = pl.ds(half * HD + off, n)
                part = dot(f0, w[0, :, cols]) + dot(f1, w[1, :, cols])
                rb[half, c, :, :, :, pl.ds(off, n)] = part.astype(BF16).reshape(4, 4, 16, n)
            a, b, dev = axes(half)
            up, dn, op = lax.rem(a + 1, 4), lax.rem(a + 3, 4), lax.rem(a + 2, 4)
            send(sel(rb, half, c, op, 0, 2, cg), t1.at[half, c, 0, :, :, cg], ("r", c, g), dev(1, 0))
            send(sel(rb, half, c, op, 2, 2, cg), t1.at[half, c, 1, :, :, cg], ("r", c, g), dev(3, 0))
            send(sel(rb, half, c, up, 2, 2, cg), t2.at[half, c, 0, pl.ds(2, 2), :, cg], ("t", c, g), dev(1, 0))
            send(sel(rb, half, c, dn, 0, 2, cg), t2.at[half, c, 1, pl.ds(0, 2), :, cg], ("t", c, g), dev(3, 0))

    def st_transpose(c):
        for h in range(2):
            feat_t[h, :, pl.ds(c * CH, CH)] = feats[c, h].reshape(CH, HF).T

    def st_ring(c, g):
        cg = group(g)
        recv(("r", c, g))
        for half in range(2):
            a, b, dev = axes(half)
            up, dn = lax.rem(a + 1, 4), lax.rem(a + 3, 4)
            at = sel(rb, half, c, up, 0, 2, cg)
            at[...] = (at[...].astype(F32) + t1[half, c, 0, :, :, cg].astype(F32)).astype(BF16)
            send(at, t2.at[half, c, 0, pl.ds(0, 2), :, cg], ("t", c, g), dev(1, 0))
            at = sel(rb, half, c, dn, 2, 2, cg)
            at[...] = (at[...].astype(F32) + t1[half, c, 1, :, :, cg].astype(F32)).astype(BF16)
            send(at, t2.at[half, c, 1, pl.ds(2, 2), :, cg], ("t", c, g), dev(3, 0))

    def st_second(c, g):
        cg = group(g)
        recv(("t", c, g))
        for half in range(2):
            a, b, dev = axes(half)
            own = sel(rb, half, c, a, 0, 4, cg)
            total = (own[...].astype(F32) + t2[half, c, 0, :, :, cg].astype(F32)
                     + t2[half, c, 1, :, :, cg].astype(F32))
            qs[half, c, :, :, cg] = total
            us[half, c, :, :, cg] = total.astype(BF16)
            for j in range(1, 4):
                send(us.at[half, c, lax.rem(b + j, 4), :, cg], qr.at[half, c, j - 1, :, cg], ("q", c, g), dev(0, j))

    def st_swap(c, g):
        cg = group(g)
        recv(("q", c, g))
        for half in range(2):
            a, b, dev = axes(half)
            total = qs[half, c, b, :, cg]
            for j in range(1, 4):
                total = total + qr[half, c, j - 1, :, cg].astype(F32)
            us[half, c, b, :, cg] = total.astype(BF16)
            send(us.at[half, c, b, :, cg], ur.at[half, c, :, cg], ("u", c, g), partner_z)

    def st_residual(c, g):
        cg = group(g)
        if c == 0 and g == 0:
            recv("tgt")
        recv(("u", c, g))
        for half in range(2):
            a, b, dev = axes(half)
            cols = pl.ds(half * HD + g * GW, GW)
            total = us[half, c, b, :, cg].astype(F32) + ur[half, c, :, cg].astype(F32)
            total = total + dbias_ref[:, cols] - tg[c, :, cols].astype(F32)
            res[half, c, x, y, :, cg] = total.astype(BF16)
            mine = res.at[half, c, x, y, :, cg]
            for j in range(1, 4):
                send(mine, mine, ("a", c, g), dev(0, j))

    def st_gather(c, g):
        cg = group(g)
        recv(("a", c, g))
        for half in range(2):
            a, b, dev = axes(half)
            lo, hi = sel(res, half, c, a, 0, 2, cg), sel(res, half, c, a, 2, 2, cg)
            send(lo, lo, ("b", c, g), dev(1, 0))
            send(hi, hi, ("b", c, g), dev(3, 0))
            send(hi, hi, ("e", c, g), dev(1, 0))
            send(lo, lo, ("e", c, g), dev(3, 0))

    def st_forward(c, g):
        cg = group(g)
        recv(("b", c, g))
        for half in range(2):
            a, b, dev = axes(half)
            up, dn = lax.rem(a + 1, 4), lax.rem(a + 3, 4)
            at = sel(res, half, c, dn, 0, 2, cg)
            send(at, at, ("e", c, g), dev(1, 0))
            at = sel(res, half, c, up, 2, 2, cg)
            send(at, at, ("e", c, g), dev(3, 0))

    def st_summed(c, g):
        recv(("e", c, g))
        r = [res[half, c, :, :, :, group(g)].reshape(CH, GW) for half in range(2)]

        def half_of(h):
            return jnp.concatenate(
                [dot_nt(r[0], w[h, pl.ds(n, 256), pl.ds(g * GW, GW)])
                 + dot_nt(r[1], w[h, pl.ds(n, 256), pl.ds(HD + g * GW, GW)])
                 for n in range(0, HF, 256)], axis=1)

        if g == 0:
            xacc[...] = half_of(1 - core)
            pown[c] = half_of(core)
        elif g < NG - 1:
            xacc[...] += half_of(1 - core)
            pown[c] += half_of(core)
        else:
            xs[1, c] = (xacc[...] + half_of(1 - core)).astype(BF16)
            share_x(c, 1)
            pown[c] += half_of(core)

    def st_src_t(c):
        src_t[:, pl.ds(c * CH, CH)] = srcb[c].reshape(CH, KP).T

    def st_enc_grad(c):
        recv(("h", 1, c))
        lhs = src_t[:, pl.ds(c * CH, CH)]
        for h in range(2):
            part = dot(lhs, fgr[c, h].reshape(CH, HF))
            if c == 0:
                egacc[h] = part
            else:
                egout[:, pl.ds(h * HF, HF)] = (egacc[h] + part)[:KD].astype(BF16)

    outs = []

    def put(src, dst):
        outs.append(pltpu.make_async_copy(src, dst, lsem.at[8 + len(outs)]))
        outs[-1].start()

    def st_dec_grad(quarter):
        rows = pl.ds(quarter * 256, 256)
        lhs = feat_t[quarter // 2, pl.ds(quarter % 2 * 256, 256), :]
        for half in range(2):
            for off, n in TILES:
                rhs = res[half, :, :, :, :, pl.ds(off, n)].reshape(2 * CH, n)
                stag[rows, pl.ds(half * HD + off, n)] = dot(lhs, rhs).astype(BF16)
        put(stag.at[rows], dg_ref.at[0, rows])

    def line(c, ph):
        return [(st_line, c, ph, b) for b in range(NB)]

    def near(c, ph, *bs):
        return [(st_near, c, ph, b) for b in bs]

    def far(c, ph, *bs):
        return [(st_far, c, ph, b) for b in bs]

    def end(c, ph):
        return [(st_far_end, c, ph, b) for b in range(NB)]

    timed = []
    for k, begin in ((0, 16.5), (1, 22.2)):
        timed += [(15.0 + 2.0 * k, (st_preact, k))]
        timed += [(16.5 + 1.3 * k + 0.01 * b, line(k, 0)[b]) for b in range(NB)]
        timed += [(begin + 2.2 + 0.72 * b, near(k, 0, b)[0]) for b in range(NB)]
        timed += [(begin + 5.4 + 0.72 * b, far(k, 0, b)[0]) for b in range(NB)]
        timed += [(begin + 8.7 + 0.72 * b, end(k, 0)[b]) for b in range(NB)]
    steps = ((st_rebuilt, 0), (st_ring, 3.5), (st_second, 7.4), (st_swap, 11.2), (st_residual, 16.7),
             (st_gather, 20.5), (st_forward, 24.0), (st_summed, 27.8))
    for c, begin in ((0, 30.5), (1, 38.6)):
        for stage, lag in steps:
            timed += [(begin + lag + (1.25 if lag else 0.85) * g, (stage, c, g)) for g in range(NG)]
        ready = begin + 27.8 + 1.25 * NG
        timed += [(ready + 0.3 + 0.01 * b, line(c, 1)[b]) for b in range(NB)]
        timed += [(ready + 3.6 + 0.72 * b, near(c, 1, b)[0]) for b in range(NB)]
        timed += [(ready + 6.8 + 0.72 * b, far(c, 1, b)[0]) for b in range(NB)]
        timed += [(ready + 12.6 + 0.01 * b, end(c, 1)[b]) for b in range(NB)]
        timed += [(ready + 18, (st_enc_grad, c))]
        timed += [(begin + 5, (st_transpose, c)), (begin + 6, (st_src_t, c))]
    timed += [(ready + t, (st_dec_grad, i)) for i, t in enumerate((0.6, 2.1, 12.4, 12.41))]
    order = [entry for _, entry in sorted(timed, key=lambda item: item[0])]
    for stage, *args in order:
        now[0] = (stage.__name__, args[0])
        stage(*args)
    put(egout, eg_ref)
    for batch, n in stage_tiles.items():
        if batch[0] in ("end", "inner"):
            @pl.when(is_end if batch[0] == "end" else is_inner)
            def _():
                pltpu.make_async_copy(bulk(n), bulk(n), ssem.at[sids[batch]]).wait()
        else:
            pltpu.make_async_copy(bulk(n), bulk(n), ssem.at[sids[batch]]).wait()
    for copy in outs:
        copy.wait()
    assert len(ids.table) == N_RECV and len(sids.table) == N_SEND, (len(ids.table), len(sids.table))


def put_out(eg_in, dg_in, eg_out, dg_out, sem):
    copies = [pltpu.make_async_copy(eg_in, eg_out, sem.at[0])]
    for i in range(8):
        rows = pl.ds(i * 128, 128)
        copies.append(pltpu.make_async_copy(dg_in.at[0, rows], dg_out.at[0, rows], sem.at[i + 1]))
    for copy in copies:
        copy.start()
    for copy in copies:
        copy.wait()


def step(source, enc_weight, enc_bias, dec_weight, dec_bias, targets):
    vmem = pl.BlockSpec(memory_space=pltpu.VMEM)
    hbm = pl.BlockSpec(memory_space=pltpu.HBM)
    V = pltpu.VMEM
    grads = pl.pallas_call(
        kernel,
        out_shape=(
            jax.ShapeDtypeStruct((KD, NF), BF16),
            jax.ShapeDtypeStruct((1, NF, D), BF16),
        ),
        in_specs=[hbm] * 6,
        out_specs=(pl.BlockSpec(memory_space=pl.ANY),) * 2,
        scratch_shapes=[
            V((16, KD), BF16),
            V((1, NF), F32),
            V((1, D), F32),
            V((2, 16, 16, KP), BF16),
            V((2, KP, HF), BF16),
            V((2, HF, D), BF16),
            V((2, 16, D), BF16),
            V((2, CH, HF), F32),
            V((2, CH, HF), F32),
            V((CH, HF), F32),
            V((2, 2, CH, HF), BF16),
            V((2, 2, CH, HF), BF16),
            V((2, 2, 2, CH, HF), BF16),
            V((2, 2, CH, HF), BF16),
            V((2, 2, CH, HF), BF16),
            V((2, CH, HF), F32),
            V((2, 2, NB, RB, HF), BF16),
            V((2, HF, 2 * CH), BF16),
            V((KP, 2 * CH), BF16),
            V((2, 2, NB, RB, HF), BF16),
            V((2, KP, HF), F32),
            V((2, 2, 4, 4, 16, HD), BF16),
            V((2, 2, 2, 2, 16, HD), BF16),
            V((2, 2, 2, 4, 16, HD), BF16),
            V((2, 2, 4, 16, HD), F32),
            V((2, 2, 3, 16, HD), BF16),
            V((2, 2, 4, 16, HD), BF16),
            V((2, 2, 16, HD), BF16),
            V((2, 2, 4, 4, 16, HD), BF16),
            V((2, 2, 16, HD), BF16),
            V((NF, D), BF16),
            V((KD, NF), BF16),
            pltpu.SemaphoreType.DMA((N_SEND,)),
            pltpu.SemaphoreType.DMA((N_RECV,)),
            pltpu.SemaphoreType.DMA((13,)),
        ],
        compiler_params=pltpu.CompilerParams(
            collective_id=0, has_side_effects=True, vmem_limit_bytes=48 * 1024 * 1024),
    )(*[pltpu.with_memory_space_constraint(a, pltpu.HBM)
        for a in (source, enc_weight, enc_bias.reshape(1, NF), dec_weight, dec_bias, targets)])
    anywhere = pl.BlockSpec(memory_space=pl.ANY)
    return pl.pallas_call(
        put_out,
        out_shape=tuple(jax.ShapeDtypeStruct(g.shape, g.dtype) for g in grads),
        in_specs=[anywhere] * 2,
        out_specs=(anywhere,) * 2,
        scratch_shapes=[pltpu.SemaphoreType.DMA((9,))],
        compiler_params=pltpu.CompilerParams(vmem_limit_bytes=1024 * 1024),
    )(*grads)


def solution(mesh):
    placed = (
        P("feat", "layer"),
        P("layer", "feat"),
        P("feat"),
        P("layer", "feat", None),
        P("layer", None),
        P("layer", "feat", None),
    )
    return jax.shard_map(
        step,
        mesh=mesh,
        in_specs=placed,
        out_specs=(P("layer", "feat"), P("layer", "feat", None)),
        check_vma=False,
    )
```

```python
import math

import jax
import jax.numpy as jnp
from jax import lax
from jax.experimental import pallas as pl
from jax.experimental.pallas import tpu as pltpu
from jax.sharding import PartitionSpec as P

MESH = pl.DeviceIdType.MESH
F32 = jnp.float32
BF16 = jnp.bfloat16

D = 2304
HD = D // 2
NF = 1024
HF = NF // 2
KD = 288
KP = 384
CH = 256
GROUPS = ((0, 384), (384, 384), (768, 384))
NG = len(GROUPS)
NB = 8
RB = CH // NB
TILES = ((0, 256), (256, 256), (512, 256), (768, 256), (1024, 128))


OFFSETS = [(dx, dy) for dx in range(4) for dy in range(4) if dx or dy]


def hops(offset):
    return sum(min(d, 4 - d) for d in offset)


def dot(a, b):
    return jnp.dot(a, b, preferred_element_type=F32)


def dot_nt(a, b):
    return lax.dot_general(a, b, (((1,), (1,)), ((), ())), preferred_element_type=F32)


class Ids:
    def __init__(self):
        self.table = {}

    def __getitem__(self, name):
        return self.table.setdefault(name, len(self.table))


N_RECV = 122
N_SEND = 29


def kernel(src_hbm, encw_ref, bias_hbm, decw_ref, dbias_hbm, tgt_hbm, eg_ref, dg_ref,
           src_ref, bias_ref, dbias_ref,
           srcb, wenc, w, tg, pown, acc, xacc, xs, xr, ls, nb, fb, act, feats, feat_t, src_t, fgr, egacc,
           rb, t1, t2, qs, qr, us, ur, res, rl, stag, egout, ssem, rsem, lsem):
    layer = lax.axis_index("layer")
    feat = lax.axis_index("feat")
    core, zl = lax.rem(layer, 2), lax.div(layer, 2)
    zh = lax.rem(feat, 2)
    y = lax.rem(lax.div(feat, 2), 4)
    x = lax.div(feat, 8)

    def feat_of(xx, yy, zz):
        return (lax.rem(xx, 4) * 4 + lax.rem(yy, 4)) * 2 + zz

    def xy_dev(dx, dy):
        return {"layer": layer, "feat": feat_of(x + dx, y + dy, zh)}

    partner_z = {"layer": layer, "feat": feat_of(x, y, 1 - zh)}
    partner_c = {"layer": zl * 2 + 1 - core, "feat": feat}

    def ring_dev(d):
        z = lax.rem(zh * 4 + zl + 8 + d, 8)
        return {"layer": lax.rem(z, 4) * 2 + core, "feat": feat_of(x, y, lax.div(z, 4))}

    ids, sids = Ids(), Ids()
    tiles, stage_tiles, now = {}, {}, ["start"]

    def bulk(n):
        wide = max(k for k in range(1, 19) if n % k == 0 and n // k <= 32)
        return w.at[0, pl.ds(0, n // wide * 16), pl.ds(0, wide * 128)]

    def count(ref):
        return math.prod(ref.shape) // 2048

    def send(src, dst, name, dev, slot=0, batch=None, tally=True):
        batch = batch or now[0]
        stage_tiles[batch] = stage_tiles.get(batch, 0) + count(src)
        if tally:
            tiles[name] = tiles.get(name, 0) + count(src)
        pltpu.make_async_remote_copy(
            src_ref=src, dst_ref=dst, send_sem=ssem.at[sids[batch]], recv_sem=rsem.at[ids[name] + slot],
            device_id=dev, device_id_type=MESH).start()

    def recv(name, slot=0, dst=None):
        if dst is None:
            dst = bulk(tiles[name])
        pltpu.make_async_copy(dst, dst, rsem.at[ids[name] + slot]).wait()

    mine_in = lax.rem(zh + x + y, 2)
    oz = 1 - mine_in

    loads = {}

    def load(name, src, dst):
        loads[name] = pltpu.make_async_copy(src, dst, lsem.at[len(loads)])
        loads[name].start()

    load("src", src_hbm, src_ref)
    load("tgt", tgt_hbm.at[0], tg.at[mine_in])
    load("bias", bias_hbm, bias_ref)
    load("dbias", dbias_hbm, dbias_ref)
    for h in range(2):
        load(("e", h), encw_ref.at[:, pl.ds(h * HF, HF)], wenc.at[h, pl.ds(0, KD)])
    for h in range(2):
        load(("d", h), decw_ref.at[0, pl.ds(h * HF, HF)], w.at[h])

    barrier = pltpu.get_barrier_semaphore()
    peers = [xy_dev(dx, dy) for dx, dy in OFFSETS]
    peers += [partner_z, partner_c] + [ring_dev(d) for d in (1, -1, 3, -3)]
    for dev in peers:
        pl.semaphore_signal(barrier, inc=1, device_id=dev, device_id_type=MESH)

    me = x * 4 + y
    zero = jnp.zeros((16, KP - KD), BF16)
    loads['src'].wait()
    srcb[mine_in, me] = jnp.concatenate([src_ref[...], zero], axis=1)
    for h in range(2):
        wenc[h, pl.ds(KD, KP - KD)] = jnp.zeros((KP - KD, HF), BF16)
    pl.semaphore_wait(barrier, len(peers))

    for i in range(2):
        ids[("src", i)]
    send(srcb.at[mine_in, me], srcb.at[mine_in, me], "srcz", partner_z)

    def spread(z, batch):
        for dx, dy in sorted(OFFSETS, key=lambda o: -hops(o)):
            send(srcb.at[z, me], srcb.at[z, me], ("src", 0), xy_dev(dx, dy), z, batch=batch)

    @pl.when(mine_in == 0)
    def _():
        spread(mine_in, "own")

    recv("srcz")
    now[0] = "relay"
    spread(oz, "relay")

    @pl.when(mine_in == 1)
    def _():
        spread(mine_in, "own")

    tiles[("src", 0)] //= 3
    stage_tiles["own"] //= 2
    for name in ("tgt", "bias", "dbias"):
        loads[name].wait()
    send(tg.at[mine_in], tg.at[mine_in], "tgt", partner_z)

    is_end = (zl == 0) | (zl == 3)
    is_inner = (zl == 1) | (zl == 2)
    toward = 1 - 2 * lax.div(zl, 2)
    far_dev = {"layer": lax.rem(zl + toward + 4, 4) * 2 + core, "feat": feat}
    near_dev = {"layer": lax.rem(zl - toward + 4, 4) * 2 + core, "feat": feat}

    def share_x(c, ph):
        for b in range(2):
            rows = pl.ds(b * 128, 128)
            send(xs.at[ph, c, rows], xr.at[ph, c, rows], ("x", ph, c, b), partner_c)

    def layer_sum_start(c, ph, half_of):
        xs[ph, c] = half_of(1 - core).astype(BF16)
        share_x(c, ph)
        pown[c] = half_of(core)

    def line_start(c, ph, b):
        rows = pl.ds(b * RB, RB)
        if b % (NB // 2) == 0:
            recv(("x", ph, c, b // (NB // 2)))
        own = pown[c, rows] + xr[ph, c, rows].astype(F32)
        pown[c, rows] = own
        acc[c, rows] = own
        ids[("n", ph, c, b)], ids[("f", ph, c, b)]

        @pl.when(is_end)
        def _():
            ls[0, ph, c, rows] = own.astype(BF16)
            send(ls.at[0, ph, c, rows], nb.at[ph, c, rows], ("n", ph, c, b), far_dev, batch=("end", ph, c))

    def line_near(c, ph, b):
        rows = pl.ds(b * RB, RB)

        @pl.when(is_inner)
        def _():
            recv(("n", ph, c, b), dst=nb.at[ph, c, rows])
            both = acc[c, rows] + nb[ph, c, rows].astype(F32)
            acc[c, rows] = both
            ls[0, ph, c, rows] = both.astype(BF16)
            send(ls.at[0, ph, c, rows], fb.at[ph, c, rows], ("f", ph, c, b), far_dev, batch=("inner", ph, c))

    def line_far(c, ph, b, inner):
        rows = pl.ds(b * RB, RB)
        batch = ("inner" if inner else "end", ph, c)

        @pl.when(is_inner if inner else is_end)
        def _():
            recv(("f", ph, c, b), dst=fb.at[ph, c, rows])
            beyond = fb[ph, c, rows].astype(F32)
            if inner:
                ls[1, ph, c, rows] = (pown[c, rows] + beyond).astype(BF16)
                send(ls.at[1, ph, c, rows], fb.at[ph, c, rows], ("f", ph, c, b), near_dev, batch=batch)
            total = acc[c, rows] + beyond
            if ph == 0:
                bias = bias_ref[:, pl.ds(pl.multiple_of(core * HF, HF), HF)]
                active = jnp.maximum(total + bias, 0.0)
                act[c, rows] = active
                feats[c, core, b] = (active * active).astype(BF16)
                mine = feats.at[c, core, b]
            else:
                fgr[c, core, b] = (2.0 * act[c, rows] * total).astype(BF16)
                mine = fgr.at[c, core, b]
            send(mine, mine, ("h", ph, c), partner_c, batch=batch, tally=inner)

    def st_preact(k):
        recv(("src", 0), k)
        if k == 0:
            loads[("e", 0)].wait()
            loads[("e", 1)].wait()
        rows = srcb[k].reshape(CH, KP)
        layer_sum_start(k, 0, lambda h: dot(rows, wenc[h]))

    def st_line(c, ph, b):
        line_start(c, ph, b)

    def st_near(c, ph, b):
        line_near(c, ph, b)

    def st_far(c, ph, b):
        line_far(c, ph, b, True)

    def st_far_end(c, ph, b):
        line_far(c, ph, b, False)

    def axes(half):
        if half == 0:
            return x, y, (lambda da, db: xy_dev(da, db))
        return y, x, (lambda da, db: xy_dev(db, da))

    def sel(ref, half, c, a, b, nb, cols):
        if half == 0:
            return ref.at[half, c, a, pl.ds(b, nb), :, cols]
        return ref.at[half, c, pl.ds(b, nb), a, :, cols]

    def tiles_of(g):
        start, width = GROUPS[g]
        return [(start + t, min(256, width - t)) for t in range(0, width, 256)]

    def group(g):
        return pl.ds(*GROUPS[g])

    def st_rebuilt(c, g):
        if g == 0:
            recv(("h", 0, c))
        if g == 0 and c == 0:
            loads[("d", 0)].wait()
            loads[("d", 1)].wait()
        f0 = feats[c, 0].reshape(CH, HF)
        f1 = feats[c, 1].reshape(CH, HF)
        cg = group(g)
        for half in range(2):
            for off, n in tiles_of(g):
                cols = pl.ds(half * HD + off, n)
                part = dot(f0, w[0, :, cols]) + dot(f1, w[1, :, cols])
                rb[half, c, :, :, :, pl.ds(off, n)] = part.astype(BF16).reshape(4, 4, 16, n)
            a, b, dev = axes(half)
            up, dn, op = lax.rem(a + 1, 4), lax.rem(a + 3, 4), lax.rem(a + 2, 4)
            send(sel(rb, half, c, op, 0, 2, cg), t1.at[half, c, 0, :, :, cg], ("r", c, g), dev(1, 0))
            send(sel(rb, half, c, op, 2, 2, cg), t1.at[half, c, 1, :, :, cg], ("r", c, g), dev(3, 0))
            send(sel(rb, half, c, up, 2, 2, cg), t2.at[half, c, 0, pl.ds(2, 2), :, cg], ("t", c, g), dev(1, 0))
            send(sel(rb, half, c, dn, 0, 2, cg), t2.at[half, c, 1, pl.ds(0, 2), :, cg], ("t", c, g), dev(3, 0))

    def st_transpose(c):
        for h in range(2):
            feat_t[h, :, pl.ds(c * CH, CH)] = feats[c, h].reshape(CH, HF).T

    def st_ring(c, g):
        cg = group(g)
        recv(("r", c, g))
        for half in range(2):
            a, b, dev = axes(half)
            up, dn = lax.rem(a + 1, 4), lax.rem(a + 3, 4)
            at = sel(rb, half, c, up, 0, 2, cg)
            at[...] = (at[...].astype(F32) + t1[half, c, 0, :, :, cg].astype(F32)).astype(BF16)
            send(at, t2.at[half, c, 0, pl.ds(0, 2), :, cg], ("t", c, g), dev(1, 0))
            at = sel(rb, half, c, dn, 2, 2, cg)
            at[...] = (at[...].astype(F32) + t1[half, c, 1, :, :, cg].astype(F32)).astype(BF16)
            send(at, t2.at[half, c, 1, pl.ds(2, 2), :, cg], ("t", c, g), dev(3, 0))

    def st_second(c, g):
        cg = group(g)
        recv(("t", c, g))
        for half in range(2):
            a, b, dev = axes(half)
            own = sel(rb, half, c, a, 0, 4, cg)
            total = (own[...].astype(F32) + t2[half, c, 0, :, :, cg].astype(F32)
                     + t2[half, c, 1, :, :, cg].astype(F32))
            qs[half, c, :, :, cg] = total
            us[half, c, :, :, cg] = total.astype(BF16)
            for j in (2, 1, 3):
                send(us.at[half, c, lax.rem(b + j, 4), :, cg], qr.at[half, c, j - 1, :, cg], ("q", c, g), dev(0, j))

    def st_swap(c, g):
        cg = group(g)
        recv(("q", c, g))
        for half in range(2):
            a, b, dev = axes(half)
            total = qs[half, c, b, :, cg]
            for j in range(1, 4):
                total = total + qr[half, c, j - 1, :, cg].astype(F32)
            us[half, c, b, :, cg] = total.astype(BF16)
            send(us.at[half, c, b, :, cg], ur.at[half, c, :, cg], ("u", c, g), partner_z)

    def st_residual(c, g):
        cg = group(g)
        if c == 0 and g == 0:
            recv("tgt")
        recv(("u", c, g))
        for half in range(2):
            a, b, dev = axes(half)
            cols = pl.ds(half * HD + GROUPS[g][0], GROUPS[g][1])
            total = us[half, c, b, :, cg].astype(F32) + ur[half, c, :, cg].astype(F32)
            total = total + dbias_ref[:, cols] - tg[c, :, cols].astype(F32)
            res[half, c, x, y, :, cg] = total.astype(BF16)
            mine = res.at[half, c, x, y, :, cg]
            for j in (2, 1, 3):
                send(mine, mine, ("a", c, g), dev(0, j))

    def st_gather(c, g):
        cg = group(g)
        recv(("a", c, g))
        for half in range(2):
            a, b, dev = axes(half)
            lo, hi = sel(res, half, c, a, 0, 2, cg), sel(res, half, c, a, 2, 2, cg)
            send(lo, lo, ("b", c, g), dev(1, 0))
            send(hi, hi, ("b", c, g), dev(3, 0))
            send(hi, hi, ("e", c, g), dev(1, 0))
            send(lo, lo, ("e", c, g), dev(3, 0))

    def st_forward(c, g):
        cg = group(g)
        recv(("b", c, g))
        for half in range(2):
            a, b, dev = axes(half)
            up, dn = lax.rem(a + 1, 4), lax.rem(a + 3, 4)
            at = sel(res, half, c, dn, 0, 2, cg)
            send(at, at, ("e", c, g), dev(1, 0))
            at = sel(res, half, c, up, 2, 2, cg)
            send(at, at, ("e", c, g), dev(3, 0))

    def st_summed(c, g):
        recv(("e", c, g))
        start, width = GROUPS[g]
        r = [res[half, c, :, :, :, group(g)].reshape(CH, width) for half in range(2)]

        def half_of(h):
            return jnp.concatenate(
                [dot_nt(r[0], w[h, pl.ds(n, 256), pl.ds(start, width)])
                 + dot_nt(r[1], w[h, pl.ds(n, 256), pl.ds(HD + start, width)])
                 for n in range(0, HF, 256)], axis=1)

        if g == 0:
            xacc[...] = half_of(1 - core)
            pown[c] = half_of(core)
        elif g < NG - 1:
            xacc[...] += half_of(1 - core)
            pown[c] += half_of(core)
        else:
            xs[1, c] = (xacc[...] + half_of(1 - core)).astype(BF16)
            share_x(c, 1)
            pown[c] += half_of(core)

    def st_src_t(c):
        src_t[:, pl.ds(c * CH, CH)] = srcb[c].reshape(CH, KP).T

    def st_enc_grad(c):
        recv(("h", 1, c))
        lhs = src_t[:, pl.ds(c * CH, CH)]
        for h in range(2):
            part = dot(lhs, fgr[c, h].reshape(CH, HF))
            if c == 0:
                egacc[h] = part
            else:
                egout[:, pl.ds(h * HF, HF)] = (egacc[h] + part)[:KD].astype(BF16)

    outs = []

    def put(src, dst):
        outs.append(pltpu.make_async_copy(src, dst, lsem.at[8 + len(outs)]))
        outs[-1].start()

    def st_dec_grad(quarter):
        rows = pl.ds(quarter * 256, 256)
        lhs = feat_t[quarter // 2, pl.ds(quarter % 2 * 256, 256), :]
        for half in range(2):
            for off, n in TILES:
                rhs = res[half, :, :, :, :, pl.ds(off, n)].reshape(2 * CH, n)
                stag[rows, pl.ds(half * HD + off, n)] = dot(lhs, rhs).astype(BF16)
        put(stag.at[rows], dg_ref.at[0, rows])

    def line(c, ph):
        return [(st_line, c, ph, b) for b in range(NB)]

    def near(c, ph, *bs):
        return [(st_near, c, ph, b) for b in bs]

    def far(c, ph, *bs):
        return [(st_far, c, ph, b) for b in bs]

    def end(c, ph):
        return [(st_far_end, c, ph, b) for b in range(NB)]

    timed = []
    for k, begin in ((0, 15.0), (1, 20.7)):
        timed += [(13.5 + 2.0 * k, (st_preact, k))]
        timed += [(15.0 + 1.3 * k + 0.01 * b, line(k, 0)[b]) for b in range(NB)]
        timed += [(begin + 2.2 + 0.72 * b, near(k, 0, b)[0]) for b in range(NB)]
        timed += [(begin + 5.4 + 0.72 * b, far(k, 0, b)[0]) for b in range(NB)]
        timed += [(begin + 8.7 + 0.72 * b, end(k, 0)[b]) for b in range(NB)]
    steps = ((st_rebuilt, 0), (st_ring, 3.5), (st_second, 7.4), (st_swap, 11.2), (st_residual, 16.7),
             (st_gather, 20.5), (st_forward, 24.0), (st_summed, 27.8))
    for c, begin in ((0, 29.0), (1, 35.5)):
        for stage, lag in steps:
            timed += [(begin + lag + (1.25 if lag else 0.85) * g, (stage, c, g)) for g in range(NG)]
        ready = begin + 27.8 + 1.25 * NG
        timed += [(ready + 0.3 + 0.01 * b, line(c, 1)[b]) for b in range(NB)]
        timed += [(ready + 3.6 + 0.72 * b, near(c, 1, b)[0]) for b in range(NB)]
        timed += [(ready + 6.8 + 0.72 * b, far(c, 1, b)[0]) for b in range(NB)]
        timed += [(ready + 12.6 + 0.01 * b, end(c, 1)[b]) for b in range(NB)]
        timed += [(ready + 18, (st_enc_grad, c))]
        timed += [(begin + 5, (st_transpose, c)), (begin + 6, (st_src_t, c))]
    timed += [(ready + t, (st_dec_grad, i)) for i, t in enumerate((0.6, 2.1, 12.4, 12.41))]
    order = [entry for _, entry in sorted(timed, key=lambda item: item[0])]
    for stage, *args in order:
        now[0] = (stage.__name__, args[0])
        stage(*args)
    put(egout, eg_ref)
    for batch, n in stage_tiles.items():
        if batch[0] in ("end", "inner"):
            @pl.when(is_end if batch[0] == "end" else is_inner)
            def _():
                pltpu.make_async_copy(bulk(n), bulk(n), ssem.at[sids[batch]]).wait()
        else:
            pltpu.make_async_copy(bulk(n), bulk(n), ssem.at[sids[batch]]).wait()
    for copy in outs:
        copy.wait()
    assert len(ids.table) == N_RECV and len(sids.table) == N_SEND, (len(ids.table), len(sids.table))


def put_out(eg_in, dg_in, eg_out, dg_out, sem):
    copies = [pltpu.make_async_copy(eg_in, eg_out, sem.at[0])]
    for i in range(8):
        rows = pl.ds(i * 128, 128)
        copies.append(pltpu.make_async_copy(dg_in.at[0, rows], dg_out.at[0, rows], sem.at[i + 1]))
    for copy in copies:
        copy.start()
    for copy in copies:
        copy.wait()


def step(source, enc_weight, enc_bias, dec_weight, dec_bias, targets):
    vmem = pl.BlockSpec(memory_space=pltpu.VMEM)
    hbm = pl.BlockSpec(memory_space=pltpu.HBM)
    V = pltpu.VMEM
    grads = pl.pallas_call(
        kernel,
        out_shape=(
            jax.ShapeDtypeStruct((KD, NF), BF16),
            jax.ShapeDtypeStruct((1, NF, D), BF16),
        ),
        in_specs=[hbm] * 6,
        out_specs=(pl.BlockSpec(memory_space=pl.ANY),) * 2,
        scratch_shapes=[
            V((16, KD), BF16),
            V((1, NF), F32),
            V((1, D), F32),
            V((2, 16, 16, KP), BF16),
            V((2, KP, HF), BF16),
            V((2, HF, D), BF16),
            V((2, 16, D), BF16),
            V((2, CH, HF), F32),
            V((2, CH, HF), F32),
            V((CH, HF), F32),
            V((2, 2, CH, HF), BF16),
            V((2, 2, CH, HF), BF16),
            V((2, 2, 2, CH, HF), BF16),
            V((2, 2, CH, HF), BF16),
            V((2, 2, CH, HF), BF16),
            V((2, CH, HF), F32),
            V((2, 2, NB, RB, HF), BF16),
            V((2, HF, 2 * CH), BF16),
            V((KP, 2 * CH), BF16),
            V((2, 2, NB, RB, HF), BF16),
            V((2, KP, HF), F32),
            V((2, 2, 4, 4, 16, HD), BF16),
            V((2, 2, 2, 2, 16, HD), BF16),
            V((2, 2, 2, 4, 16, HD), BF16),
            V((2, 2, 4, 16, HD), F32),
            V((2, 2, 3, 16, HD), BF16),
            V((2, 2, 4, 16, HD), BF16),
            V((2, 2, 16, HD), BF16),
            V((2, 2, 4, 4, 16, HD), BF16),
            V((2, 2, 16, HD), BF16),
            V((NF, D), BF16),
            V((KD, NF), BF16),
            pltpu.SemaphoreType.DMA((N_SEND,)),
            pltpu.SemaphoreType.DMA((N_RECV,)),
            pltpu.SemaphoreType.DMA((13,)),
        ],
        compiler_params=pltpu.CompilerParams(
            collective_id=0, has_side_effects=True, vmem_limit_bytes=48 * 1024 * 1024),
    )(*[pltpu.with_memory_space_constraint(a, pltpu.HBM)
        for a in (source, enc_weight, enc_bias.reshape(1, NF), dec_weight, dec_bias, targets)])
    anywhere = pl.BlockSpec(memory_space=pl.ANY)
    return pl.pallas_call(
        put_out,
        out_shape=tuple(jax.ShapeDtypeStruct(g.shape, g.dtype) for g in grads),
        in_specs=[anywhere] * 2,
        out_specs=(anywhere,) * 2,
        scratch_shapes=[pltpu.SemaphoreType.DMA((9,))],
        compiler_params=pltpu.CompilerParams(vmem_limit_bytes=1024 * 1024),
    )(*grads)


def solution(mesh):
    placed = (
        P("feat", "layer"),
        P("layer", "feat"),
        P("feat"),
        P("layer", "feat", None),
        P("layer", None),
        P("layer", "feat", None),
    )
    return jax.shard_map(
        step,
        mesh=mesh,
        in_specs=placed,
        out_specs=(P("layer", "feat"), P("layer", "feat", None)),
        check_vma=False,
    )
```

```python
import math

import jax
import jax.numpy as jnp
from jax import lax
from jax.experimental import pallas as pl
from jax.experimental.pallas import tpu as pltpu
from jax.sharding import PartitionSpec as P

MESH = pl.DeviceIdType.MESH
F32 = jnp.float32
BF16 = jnp.bfloat16

D = 2304
HD = D // 2
NF = 1024
HF = NF // 2
KD = 288
KP = 384
CH = 256
GROUPS = ((0, 384), (384, 384), (768, 384))
NG = len(GROUPS)
NB = 8
RB = CH // NB
TILES = ((0, 256), (256, 256), (512, 256), (768, 256), (1024, 128))


OFFSETS = [(dx, dy) for dx in range(4) for dy in range(4) if dx or dy]


def hops(offset):
    return sum(min(d, 4 - d) for d in offset)


def dot(a, b):
    return jnp.dot(a, b, preferred_element_type=F32)


def dot_nt(a, b):
    return lax.dot_general(a, b, (((1,), (1,)), ((), ())), preferred_element_type=F32)


class Ids:
    def __init__(self):
        self.table = {}

    def __getitem__(self, name):
        if name[0] in ("x", "n", "h"):
            name = name[:1] + name[2:]
        return self.table.setdefault(name, len(self.table))


N_RECV = 100
N_SEND = 29


def kernel(src_hbm, encw_ref, bias_hbm, decw_ref, dbias_hbm, tgt_hbm, eg_ref, dg_ref,
           src_ref, bias_ref, dbias_ref,
           srcb, wenc, w, tg, pown, acc, xacc, xs, xr, ls, nb, fb, act, feats, feat_t, src_t, fgr, egacc,
           rb, t1, t2, qs, qr, us, ur, res, rl, stag, egout, ssem, rsem, lsem):
    layer = lax.axis_index("layer")
    feat = lax.axis_index("feat")
    core, zl = lax.rem(layer, 2), lax.div(layer, 2)
    zh = lax.rem(feat, 2)
    y = lax.rem(lax.div(feat, 2), 4)
    x = lax.div(feat, 8)

    def feat_of(xx, yy, zz):
        return (lax.rem(xx, 4) * 4 + lax.rem(yy, 4)) * 2 + zz

    def xy_dev(dx, dy):
        return {"layer": layer, "feat": feat_of(x + dx, y + dy, zh)}

    partner_z = {"layer": layer, "feat": feat_of(x, y, 1 - zh)}
    partner_c = {"layer": zl * 2 + 1 - core, "feat": feat}

    def ring_dev(d):
        z = lax.rem(zh * 4 + zl + 8 + d, 8)
        return {"layer": lax.rem(z, 4) * 2 + core, "feat": feat_of(x, y, lax.div(z, 4))}

    ids, sids = Ids(), Ids()
    tiles, stage_tiles, now = {}, {}, ["start"]

    def bulk(n):
        wide = max(k for k in range(1, 19) if n % k == 0 and n // k <= 32)
        return w.at[0, pl.ds(0, n // wide * 16), pl.ds(0, wide * 128)]

    def count(ref):
        return math.prod(ref.shape) // 2048

    def send(src, dst, name, dev, slot=0, batch=None, tally=True):
        batch = batch or now[0]
        stage_tiles[batch] = stage_tiles.get(batch, 0) + count(src)
        if tally:
            tiles[name] = tiles.get(name, 0) + count(src)
        pltpu.make_async_remote_copy(
            src_ref=src, dst_ref=dst, send_sem=ssem.at[sids[batch]], recv_sem=rsem.at[ids[name] + slot],
            device_id=dev, device_id_type=MESH).start()

    def recv(name, slot=0, dst=None):
        if dst is None:
            dst = bulk(tiles[name])
        pltpu.make_async_copy(dst, dst, rsem.at[ids[name] + slot]).wait()

    mine_in = lax.rem(zh + x + y, 2)
    oz = 1 - mine_in

    loads = {}

    def load(name, src, dst):
        loads[name] = pltpu.make_async_copy(src, dst, lsem.at[len(loads)])
        loads[name].start()

    load("src", src_hbm, src_ref)
    load("tgt", tgt_hbm.at[0], tg.at[mine_in])
    load("bias", bias_hbm, bias_ref)
    load("dbias", dbias_hbm, dbias_ref)
    for h in range(2):
        load(("e", h), encw_ref.at[:, pl.ds(h * HF, HF)], wenc.at[h, pl.ds(0, KD)])
    for h in range(2):
        load(("d", h), decw_ref.at[0, pl.ds(h * HF, HF)], w.at[h])

    barrier = pltpu.get_barrier_semaphore()
    peers = [xy_dev(dx, dy) for dx, dy in OFFSETS]
    peers += [partner_z, partner_c] + [ring_dev(d) for d in (1, -1, 3, -3)]
    for dev in peers:
        pl.semaphore_signal(barrier, inc=1, device_id=dev, device_id_type=MESH)

    me = x * 4 + y
    zero = jnp.zeros((16, KP - KD), BF16)
    loads['src'].wait()
    srcb[mine_in, me] = jnp.concatenate([src_ref[...], zero], axis=1)
    for h in range(2):
        wenc[h, pl.ds(KD, KP - KD)] = jnp.zeros((KP - KD, HF), BF16)
    pl.semaphore_wait(barrier, len(peers))

    for i in range(2):
        ids[("src", i)]
    send(srcb.at[mine_in, me], srcb.at[mine_in, me], "srcz", partner_z)

    def spread(z, batch):
        for dx, dy in sorted(OFFSETS, key=lambda o: -hops(o)):
            send(srcb.at[z, me], srcb.at[z, me], ("src", 0), xy_dev(dx, dy), z, batch=batch)

    @pl.when(mine_in == 0)
    def _():
        spread(mine_in, "own")

    recv("srcz")
    now[0] = "relay"
    spread(oz, "relay")

    @pl.when(mine_in == 1)
    def _():
        spread(mine_in, "own")

    tiles[("src", 0)] //= 3
    stage_tiles["own"] //= 2
    for name in ("tgt", "bias", "dbias"):
        loads[name].wait()
    send(tg.at[mine_in], tg.at[mine_in], "tgt", partner_z)

    is_end = (zl == 0) | (zl == 3)
    is_inner = (zl == 1) | (zl == 2)
    toward = 1 - 2 * lax.div(zl, 2)
    far_dev = {"layer": lax.rem(zl + toward + 4, 4) * 2 + core, "feat": feat}
    near_dev = {"layer": lax.rem(zl - toward + 4, 4) * 2 + core, "feat": feat}

    def share_x(c, ph):
        for b in range(2):
            rows = pl.ds(b * 128, 128)
            send(xs.at[ph, c, rows], xr.at[ph, c, rows], ("x", ph, c, b), partner_c)

    def layer_sum_start(c, ph, half_of):
        xs[ph, c] = half_of(1 - core).astype(BF16)
        share_x(c, ph)
        pown[c] = half_of(core)

    def line_start(c, ph, b):
        rows = pl.ds(b * RB, RB)
        if b % (NB // 2) == 0:
            recv(("x", ph, c, b // (NB // 2)))
        own = pown[c, rows] + xr[ph, c, rows].astype(F32)
        pown[c, rows] = own
        acc[c, rows] = own
        ids[("n", ph, c, b)], ids[("f", ph, c, b)]

        @pl.when(is_end)
        def _():
            ls[0, ph, c, rows] = own.astype(BF16)
            send(ls.at[0, ph, c, rows], nb.at[ph, c, rows], ("n", ph, c, b), far_dev, batch=("end", ph, c))

    def line_near(c, ph, b):
        rows = pl.ds(b * RB, RB)

        @pl.when(is_inner)
        def _():
            recv(("n", ph, c, b), dst=nb.at[ph, c, rows])
            both = acc[c, rows] + nb[ph, c, rows].astype(F32)
            acc[c, rows] = both
            ls[0, ph, c, rows] = both.astype(BF16)
            send(ls.at[0, ph, c, rows], fb.at[ph, c, rows], ("f", ph, c, b), far_dev, batch=("inner", ph, c))

    def line_far(c, ph, b, inner):
        rows = pl.ds(b * RB, RB)
        batch = ("inner" if inner else "end", ph, c)

        @pl.when(is_inner if inner else is_end)
        def _():
            recv(("f", ph, c, b), dst=fb.at[ph, c, rows])
            beyond = fb[ph, c, rows].astype(F32)
            if inner:
                ls[1, ph, c, rows] = (pown[c, rows] + beyond).astype(BF16)
                send(ls.at[1, ph, c, rows], fb.at[ph, c, rows], ("f", ph, c, b), near_dev, batch=batch)
            total = acc[c, rows] + beyond
            if ph == 0:
                bias = bias_ref[:, pl.ds(pl.multiple_of(core * HF, HF), HF)]
                active = jnp.maximum(total + bias, 0.0)
                act[c, rows] = active
                feats[c, core, b] = (active * active).astype(BF16)
                mine = feats.at[c, core, b]
            else:
                fgr[c, core, b] = (2.0 * act[c, rows] * total).astype(BF16)
                mine = fgr.at[c, core, b]
            send(mine, mine, ("h", ph, c), partner_c, batch=batch, tally=inner)

    def st_preact(k):
        recv(("src", 0), k)
        if k == 0:
            loads[("e", 0)].wait()
            loads[("e", 1)].wait()
        rows = srcb[k].reshape(CH, KP)
        layer_sum_start(k, 0, lambda h: dot(rows, wenc[h]))

    def st_line(c, ph, b):
        line_start(c, ph, b)

    def st_near(c, ph, b):
        line_near(c, ph, b)

    def st_far(c, ph, b):
        line_far(c, ph, b, True)

    def st_far_end(c, ph, b):
        line_far(c, ph, b, False)

    def axes(half):
        if half == 0:
            return x, y, (lambda da, db: xy_dev(da, db))
        return y, x, (lambda da, db: xy_dev(db, da))

    def sel(ref, half, c, a, b, nb, cols):
        if half == 0:
            return ref.at[half, c, a, pl.ds(b, nb), :, cols]
        return ref.at[half, c, pl.ds(b, nb), a, :, cols]

    def tiles_of(g):
        start, width = GROUPS[g]
        return [(start + t, min(256, width - t)) for t in range(0, width, 256)]

    def group(g):
        return pl.ds(*GROUPS[g])

    def st_rebuilt(c, g):
        if g == 0:
            recv(("h", 0, c))
        if g == 0 and c == 0:
            loads[("d", 0)].wait()
            loads[("d", 1)].wait()
        f0 = feats[c, 0].reshape(CH, HF)
        f1 = feats[c, 1].reshape(CH, HF)
        cg = group(g)
        for half in range(2):
            for off, n in tiles_of(g):
                cols = pl.ds(half * HD + off, n)
                part = dot(f0, w[0, :, cols]) + dot(f1, w[1, :, cols])
                rb[half, c, :, :, :, pl.ds(off, n)] = part.astype(BF16).reshape(4, 4, 16, n)
            a, b, dev = axes(half)
            up, dn, op = lax.rem(a + 1, 4), lax.rem(a + 3, 4), lax.rem(a + 2, 4)
            send(sel(rb, half, c, op, 0, 2, cg), t1.at[half, c, 0, :, :, cg], ("r", c, g), dev(1, 0))
            send(sel(rb, half, c, op, 2, 2, cg), t1.at[half, c, 1, :, :, cg], ("r", c, g), dev(3, 0))
            send(sel(rb, half, c, up, 2, 2, cg), t2.at[half, c, 0, pl.ds(2, 2), :, cg], ("t", c, g), dev(1, 0))
            send(sel(rb, half, c, dn, 0, 2, cg), t2.at[half, c, 1, pl.ds(0, 2), :, cg], ("t", c, g), dev(3, 0))

    def st_transpose(c):
        for h in range(2):
            feat_t[h, :, pl.ds(c * CH, CH)] = feats[c, h].reshape(CH, HF).T

    def st_ring(c, g):
        cg = group(g)
        recv(("r", c, g))
        for half in range(2):
            a, b, dev = axes(half)
            up, dn = lax.rem(a + 1, 4), lax.rem(a + 3, 4)
            at = sel(rb, half, c, up, 0, 2, cg)
            at[...] = (at[...].astype(F32) + t1[half, c, 0, :, :, cg].astype(F32)).astype(BF16)
            send(at, t2.at[half, c, 0, pl.ds(0, 2), :, cg], ("t", c, g), dev(1, 0))
            at = sel(rb, half, c, dn, 2, 2, cg)
            at[...] = (at[...].astype(F32) + t1[half, c, 1, :, :, cg].astype(F32)).astype(BF16)
            send(at, t2.at[half, c, 1, pl.ds(2, 2), :, cg], ("t", c, g), dev(3, 0))

    def st_second(c, g):
        cg = group(g)
        recv(("t", c, g))
        for half in range(2):
            a, b, dev = axes(half)
            own = sel(rb, half, c, a, 0, 4, cg)
            total = (own[...].astype(F32) + t2[half, c, 0, :, :, cg].astype(F32)
                     + t2[half, c, 1, :, :, cg].astype(F32))
            qs[half, c, :, :, cg] = total
            us[half, c, :, :, cg] = total.astype(BF16)
            for j in (2, 1, 3):
                send(us.at[half, c, lax.rem(b + j, 4), :, cg], qr.at[half, c, j - 1, :, cg], ("q", c, g), dev(0, j))

    def st_swap(c, g):
        cg = group(g)
        recv(("q", c, g))
        for half in range(2):
            a, b, dev = axes(half)
            total = qs[half, c, b, :, cg]
            for j in range(1, 4):
                total = total + qr[half, c, j - 1, :, cg].astype(F32)
            us[half, c, b, :, cg] = total.astype(BF16)
            send(us.at[half, c, b, :, cg], ur.at[half, c, :, cg], ("u", c, g), partner_z)

    def st_residual(c, g):
        cg = group(g)
        if c == 0 and g == 0:
            recv("tgt")
        recv(("u", c, g))
        for half in range(2):
            a, b, dev = axes(half)
            cols = pl.ds(half * HD + GROUPS[g][0], GROUPS[g][1])
            total = us[half, c, b, :, cg].astype(F32) + ur[half, c, :, cg].astype(F32)
            total = total + dbias_ref[:, cols] - tg[c, :, cols].astype(F32)
            res[half, c, x, y, :, cg] = total.astype(BF16)
            mine = res.at[half, c, x, y, :, cg]
            for j in (2, 1, 3):
                send(mine, mine, ("a", c, g), dev(0, j))

    def st_gather(c, g):
        cg = group(g)
        recv(("a", c, g))
        for half in range(2):
            a, b, dev = axes(half)
            lo, hi = sel(res, half, c, a, 0, 2, cg), sel(res, half, c, a, 2, 2, cg)
            send(lo, lo, ("b", c, g), dev(1, 0))
            send(hi, hi, ("b", c, g), dev(3, 0))
            send(hi, hi, ("e", c, g), dev(1, 0))
            send(lo, lo, ("e", c, g), dev(3, 0))

    def st_forward(c, g):
        cg = group(g)
        recv(("b", c, g))
        for half in range(2):
            a, b, dev = axes(half)
            up, dn = lax.rem(a + 1, 4), lax.rem(a + 3, 4)
            at = sel(res, half, c, dn, 0, 2, cg)
            send(at, at, ("e", c, g), dev(1, 0))
            at = sel(res, half, c, up, 2, 2, cg)
            send(at, at, ("e", c, g), dev(3, 0))

    def st_summed(c, g):
        recv(("e", c, g))
        start, width = GROUPS[g]
        r = [res[half, c, :, :, :, group(g)].reshape(CH, width) for half in range(2)]

        def half_of(h):
            return jnp.concatenate(
                [dot_nt(r[0], w[h, pl.ds(n, 256), pl.ds(start, width)])
                 + dot_nt(r[1], w[h, pl.ds(n, 256), pl.ds(HD + start, width)])
                 for n in range(0, HF, 256)], axis=1)

        if g == 0:
            xacc[...] = half_of(1 - core)
            pown[c] = half_of(core)
        elif g < NG - 1:
            xacc[...] += half_of(1 - core)
            pown[c] += half_of(core)
        else:
            xs[1, c] = (xacc[...] + half_of(1 - core)).astype(BF16)
            share_x(c, 1)
            pown[c] += half_of(core)

    def st_src_t(c):
        src_t[:, pl.ds(c * CH, CH)] = srcb[c].reshape(CH, KP).T

    def st_enc_grad(c):
        recv(("h", 1, c))
        lhs = src_t[:, pl.ds(c * CH, CH)]
        for h in range(2):
            part = dot(lhs, fgr[c, h].reshape(CH, HF))
            if c == 0:
                egacc[h] = part
            else:
                egout[:, pl.ds(h * HF, HF)] = (egacc[h] + part)[:KD].astype(BF16)

    outs = []

    def put(src, dst):
        outs.append(pltpu.make_async_copy(src, dst, lsem.at[8 + len(outs)]))
        outs[-1].start()

    def st_dec_grad(quarter):
        rows = pl.ds(quarter * 256, 256)
        lhs = feat_t[quarter // 2, pl.ds(quarter % 2 * 256, 256), :]
        for half in range(2):
            for off, n in TILES:
                rhs = res[half, :, :, :, :, pl.ds(off, n)].reshape(2 * CH, n)
                stag[rows, pl.ds(half * HD + off, n)] = dot(lhs, rhs).astype(BF16)
        put(stag.at[rows], dg_ref.at[0, rows])

    def line(c, ph):
        return [(st_line, c, ph, b) for b in range(NB)]

    def near(c, ph, *bs):
        return [(st_near, c, ph, b) for b in bs]

    def far(c, ph, *bs):
        return [(st_far, c, ph, b) for b in bs]

    def end(c, ph):
        return [(st_far_end, c, ph, b) for b in range(NB)]

    timed = []
    for k, begin in ((0, 15.0), (1, 20.7)):
        timed += [(13.5 + 2.0 * k, (st_preact, k))]
        timed += [(15.0 + 1.3 * k + 0.01 * b, line(k, 0)[b]) for b in range(NB)]
        timed += [(begin + 2.2 + 0.72 * b, near(k, 0, b)[0]) for b in range(NB)]
        timed += [(begin + 5.4 + 0.72 * b, far(k, 0, b)[0]) for b in range(NB)]
        timed += [(begin + 8.7 + 0.72 * b, end(k, 0)[b]) for b in range(NB)]
    steps = ((st_rebuilt, 0), (st_ring, 3.5), (st_second, 7.4), (st_swap, 11.2), (st_residual, 16.7),
             (st_gather, 20.5), (st_forward, 24.0), (st_summed, 27.8))
    for c, begin in ((0, 29.0), (1, 35.5)):
        for stage, lag in steps:
            timed += [(begin + lag + (1.25 if lag else 0.85) * g, (stage, c, g)) for g in range(NG)]
        ready = begin + 27.8 + 1.25 * NG
        timed += [(ready + 0.3 + 0.01 * b, line(c, 1)[b]) for b in range(NB)]
        timed += [(ready + 3.6 + 0.72 * b, near(c, 1, b)[0]) for b in range(NB)]
        timed += [(ready + 6.8 + 0.72 * b, far(c, 1, b)[0]) for b in range(NB)]
        timed += [(ready + 12.6 + 0.01 * b, end(c, 1)[b]) for b in range(NB)]
        timed += [(ready + 18, (st_enc_grad, c))]
        timed += [(begin + 5, (st_transpose, c)), (begin + 6, (st_src_t, c))]
    timed += [(ready + t, (st_dec_grad, i)) for i, t in enumerate((0.6, 2.1, 12.4, 12.41))]
    order = [entry for _, entry in sorted(timed, key=lambda item: item[0])]
    for stage, *args in order:
        now[0] = (stage.__name__, args[0])
        stage(*args)
    put(egout, eg_ref)
    for batch, n in stage_tiles.items():
        if batch[0] in ("end", "inner"):
            @pl.when(is_end if batch[0] == "end" else is_inner)
            def _():
                pltpu.make_async_copy(bulk(n), bulk(n), ssem.at[sids[batch]]).wait()
        else:
            pltpu.make_async_copy(bulk(n), bulk(n), ssem.at[sids[batch]]).wait()
    for copy in outs:
        copy.wait()
    assert len(ids.table) == N_RECV and len(sids.table) == N_SEND, (len(ids.table), len(sids.table))


def put_out(eg_in, dg_in, eg_out, dg_out, sem):
    copies = [pltpu.make_async_copy(eg_in, eg_out, sem.at[0])]
    for i in range(8):
        rows = pl.ds(i * 128, 128)
        copies.append(pltpu.make_async_copy(dg_in.at[0, rows], dg_out.at[0, rows], sem.at[i + 1]))
    for copy in copies:
        copy.start()
    for copy in copies:
        copy.wait()


def step(source, enc_weight, enc_bias, dec_weight, dec_bias, targets):
    vmem = pl.BlockSpec(memory_space=pltpu.VMEM)
    hbm = pl.BlockSpec(memory_space=pltpu.HBM)
    V = pltpu.VMEM
    grads = pl.pallas_call(
        kernel,
        out_shape=(
            jax.ShapeDtypeStruct((KD, NF), BF16),
            jax.ShapeDtypeStruct((1, NF, D), BF16),
        ),
        in_specs=[hbm] * 6,
        out_specs=(pl.BlockSpec(memory_space=pl.ANY),) * 2,
        scratch_shapes=[
            V((16, KD), BF16),
            V((1, NF), F32),
            V((1, D), F32),
            V((2, 16, 16, KP), BF16),
            V((2, KP, HF), BF16),
            V((2, HF, D), BF16),
            V((2, 16, D), BF16),
            V((2, CH, HF), F32),
            V((2, CH, HF), F32),
            V((CH, HF), F32),
            V((2, 2, CH, HF), BF16),
            V((2, 2, CH, HF), BF16),
            V((2, 2, 2, CH, HF), BF16),
            V((2, 2, CH, HF), BF16),
            V((2, 2, CH, HF), BF16),
            V((2, CH, HF), F32),
            V((2, 2, NB, RB, HF), BF16),
            V((2, HF, 2 * CH), BF16),
            V((KP, 2 * CH), BF16),
            V((2, 2, NB, RB, HF), BF16),
            V((2, KP, HF), F32),
            V((2, 2, 4, 4, 16, HD), BF16),
            V((2, 2, 2, 2, 16, HD), BF16),
            V((2, 2, 2, 4, 16, HD), BF16),
            V((2, 2, 4, 16, HD), F32),
            V((2, 2, 3, 16, HD), BF16),
            V((2, 2, 4, 16, HD), BF16),
            V((2, 2, 16, HD), BF16),
            V((2, 2, 4, 4, 16, HD), BF16),
            V((2, 2, 16, HD), BF16),
            V((NF, D), BF16),
            V((KD, NF), BF16),
            pltpu.SemaphoreType.DMA((N_SEND,)),
            pltpu.SemaphoreType.DMA((N_RECV,)),
            pltpu.SemaphoreType.DMA((13,)),
        ],
        compiler_params=pltpu.CompilerParams(
            collective_id=0, has_side_effects=True, vmem_limit_bytes=48 * 1024 * 1024),
    )(*[pltpu.with_memory_space_constraint(a, pltpu.HBM)
        for a in (source, enc_weight, enc_bias.reshape(1, NF), dec_weight, dec_bias, targets)])
    anywhere = pl.BlockSpec(memory_space=pl.ANY)
    return pl.pallas_call(
        put_out,
        out_shape=tuple(jax.ShapeDtypeStruct(g.shape, g.dtype) for g in grads),
        in_specs=[anywhere] * 2,
        out_specs=(anywhere,) * 2,
        scratch_shapes=[pltpu.SemaphoreType.DMA((9,))],
        compiler_params=pltpu.CompilerParams(vmem_limit_bytes=1024 * 1024),
    )(*grads)


def solution(mesh):
    placed = (
        P("feat", "layer"),
        P("layer", "feat"),
        P("feat"),
        P("layer", "feat", None),
        P("layer", None),
        P("layer", "feat", None),
    )
    return jax.shard_map(
        step,
        mesh=mesh,
        in_specs=placed,
        out_specs=(P("layer", "feat"), P("layer", "feat", None)),
        check_vma=False,
    )
```
